32 devices in a mesh: groups: 2 (over y), seq: 4 (over x, core), chan: 4 (over z).
Axes of the slice: x: 2, y: 2, z: 4, core: 2. Of those that a mesh axis runs over, the one named last changes fastest.
Arguments:
- gate_input: bfloat16 [1024, 4096], P(('groups', 'seq'), 'chan'), parts along dimension 0, may hold values from -6 to 6
- value_input: bfloat16 [1024, 4096], P(('groups', 'seq'), 'chan'), parts along dimension 0, may hold values from -6 to 6
- short_filter: float32 [4096, 128], P('chan'), may hold values from -0.5 to 0.5
- long_filter: bfloat16 [512, 4096], P('seq', 'chan'), may hold values from -0.375 to 0.375
- query_weight: bfloat16 [32, 128, 128], P('chan'), may hold values from -0.5 to 0.5
- key_matrix: bfloat16 [1024, 4096], P(('groups', 'seq'), 'chan'), parts along dimension 0, may hold values from -200 to 200
- value_matrix: bfloat16 [1024, 4096], P(('groups', 'seq'), 'chan'), parts along dimension 0, may hold values from -6 to 6
Outputs:
- attended: bfloat16 [1024, 4096], P(('groups', 'seq'), 'chan'), parts along dimension 0
The draws below stay inside these ranges and needn't reach their ends.
There are 2 independent parts, one for each index of `groups`. The reference program is written for one: setup_inputs(seed, part) draws one part's arguments, and reference() takes and returns one part's arrays. A program takes and returns all parts, laid end to end along the dimension named above; an argument that names none is the same for every part. Nothing has to cross between parts.
All inputs are finite; a program needn't handle non-finite values.
Results may differ from the reference program's by a relative error of at most 0.011.
Values may be sent and summed in bfloat16 or wider, within the bound.
A program may use at most 64 MiB of HBM per device.

```python
import math
import jax
import jax.numpy as jnp
from jax import lax

HEADS = 32
HEAD_DIM = 128
TAPS = 128
DW = 4096
L = 512


def draw_key_matrix(key, part):
    base = jax.random.normal(jax.random.fold_in(key, 11), (L, DW), jnp.float32)
    return jnp.clip(base, -200.0, 200.0).astype(jnp.bfloat16)


def levels(rng, shape, cuts, smallest, largest):
    factor_of, own = 1.0, jax.random.fold_in(rng, 6)
    for position, shards_of in cuts:
        draws = jnp.exp(jax.random.uniform(jax.random.fold_in(own, position), (shards_of,), jnp.float32, smallest / len(cuts), largest / len(cuts)))
        factor_of = factor_of * jnp.repeat(draws, shape[position] // shards_of).reshape([-1 if axis == position else 1 for axis in range(len(shape))])
    return factor_of


def normal_values(rng, extent, deviation, bound, cuts=(), held_as=jnp.bfloat16):
    array = jax.random.normal(rng, extent, jnp.float32) * deviation
    if len(cuts) > 0:
        array = levels(rng, extent, cuts, -0.22, 0.18) * array
    return jnp.clip(array, min=-bound, max=bound).astype(held_as)


def setup_inputs(seed: int = 0, part: int = 0) -> dict:
    seeds = jax.random.split(jax.random.key(seed), 8)
    part_splits = jax.random.split(jax.random.fold_in(seeds[7], part), 8)
    gate_input = normal_values(part_splits[0], (L, DW), 1.0, 6.0, ((0, 4), (1, 4)))
    value_input = normal_values(part_splits[1], (L, DW), 1.0, 6.0, ((0, 4), (1, 4)))
    short_filter = normal_values(seeds[2], (DW, TAPS), TAPS ** -0.5, 0.5, ((0, 4),), jnp.float32)
    long_filter = normal_values(seeds[3], (L, DW), (L // 2) ** -0.5, 0.375, ((0, 4), (1, 4)))
    query_weight = normal_values(seeds[4], (HEADS, HEAD_DIM, HEAD_DIM), HEAD_DIM ** -0.5, 0.5, ((0, 4),))
    key_matrix = draw_key_matrix(jax.random.fold_in(jax.random.fold_in(seeds[7], part), 71), part)
    value_matrix = normal_values(part_splits[6], (L, DW), 1.0, 6.0, ((0, 4), (1, 4)))
    return dict(gate_input=gate_input, value_input=value_input, short_filter=short_filter, long_filter=long_filter, query_weight=query_weight, key_matrix=key_matrix, value_matrix=value_matrix)


def reference(gate_input, value_input, short_filter, long_filter, query_weight, key_matrix, value_matrix):
    width_block = math.gcd(DW, 256)
    block_count = DW // width_block
    gate_blocks = gate_input.reshape(L, block_count, width_block).transpose(1, 0, 2)
    value_blocks = value_input.reshape(L, block_count, width_block).transpose(1, 0, 2)
    filter_blocks = short_filter.reshape(block_count, width_block, TAPS)
    long_blocks = long_filter.reshape(L, block_count, width_block).transpose(1, 0, 2)

    def one_block(quad):
        gate_part, value_part, taps_part, long_part = quad
        padded = jnp.pad(gate_part.astype(jnp.float32), ((TAPS - 1, 0), (0, 0)))
        kernel = taps_part.astype(jnp.float32)[:, ::-1].T[:, None, :]
        smoothed = lax.conv_general_dilated(padded[None], kernel, (1,), 'VALID', dimension_numbers=('NHC', 'HIO', 'NHC'), feature_group_count=width_block, precision=lax.Precision.HIGHEST)[0]
        mixed_input = (smoothed * value_part.astype(jnp.float32)).astype(jnp.bfloat16)
        spec = jnp.fft.rfft(mixed_input.astype(jnp.float32), n=2 * L, axis=0) * jnp.fft.rfft(long_part.astype(jnp.float32), n=2 * L, axis=0)
        return jnp.fft.irfft(spec, n=2 * L, axis=0)[:L].astype(jnp.bfloat16)
    conv_blocks = lax.map(one_block, (gate_blocks, value_blocks, filter_blocks, long_blocks))
    conv_out = conv_blocks.transpose(1, 0, 2).reshape(L, DW)
    conv_heads = conv_out.reshape(L, HEADS, HEAD_DIM).astype(jnp.float32)
    queries = jnp.einsum('thd,hde->the', conv_heads, query_weight.astype(jnp.float32)).astype(jnp.bfloat16)
    query_heads = queries.transpose(1, 0, 2)
    key_heads = key_matrix.reshape(L, HEADS, HEAD_DIM).transpose(1, 0, 2)
    value_heads = value_matrix.reshape(L, HEADS, HEAD_DIM).transpose(1, 0, 2)
    block_rows = math.gcd(L, 1024)

    def one_head(triple):
        head_query, head_key, head_value = triple

        def one_rows(block_pair):
            block_query, block_first = block_pair
            scores = jnp.dot(block_query, head_key.T, preferred_element_type=jnp.float32) / math.sqrt(HEAD_DIM)
            query_pos = block_first + lax.iota(jnp.int32, block_rows)
            key_pos = lax.iota(jnp.int32, L)
            allowed = key_pos[None, :] <= query_pos[:, None]
            row_peak = lax.optimization_barrier(jnp.max(jnp.where(allowed, scores, -1e+30), axis=1, keepdims=True))
            weights = jnp.where(allowed, jnp.exp(scores - row_peak), 0.0)
            weight_sum = lax.optimization_barrier(jnp.sum(weights, axis=1, keepdims=True))
            product = jnp.dot(weights.astype(jnp.bfloat16), head_value, preferred_element_type=jnp.float32)
            return (product / weight_sum).astype(jnp.bfloat16)
        block_firsts = lax.iota(jnp.int32, L // block_rows) * block_rows
        blocks = head_query.reshape(L // block_rows, block_rows, HEAD_DIM)
        return lax.map(one_rows, (blocks, block_firsts)).reshape(L, HEAD_DIM)
    result = lax.map(one_head, (query_heads, key_heads, value_heads))
    return result.transpose(1, 0, 2).reshape(L, DW)
```

```python
import functools
import math

import jax
import jax.numpy as jnp
import numpy as np
from jax import lax
from jax.experimental import pallas as pl
from jax.experimental.pallas import tpu as pltpu
from jax.sharding import PartitionSpec as P

HEAD_DIM = 128
TAPS = 128
RADIX = 128


HIGHEST = lax.Precision.HIGHEST


def shifted(value, axis, steps):
    count = lax.axis_size(axis)
    initial, last = (max(0, -steps), min(count, count - steps))
    return lax.ppermute(value, axis, [(source, source + steps) for source in range(initial, last)])


def unit_table(height, breadth, modulus, orient):
    product = (
        lax.broadcasted_iota(jnp.int32, (height, breadth), 0)
        * lax.broadcasted_iota(jnp.int32, (height, breadth), 1)
        % modulus
    )
    angles = 2.0 * math.pi / modulus * product.astype(jnp.float32)
    return (jnp.cos(angles), orient * jnp.sin(angles))


def block_table(factor, orient):
    inner_re, inner_im = unit_table(factor, factor, factor, orient)
    upper = jnp.concatenate([inner_re, inner_im], axis=1)
    lower = jnp.concatenate([-inner_im, inner_re], axis=1)
    return jnp.concatenate([upper, lower], axis=0)


def spectrum(signal, factor):
    channels, length = signal.shape
    full_length = 2 * length
    column_count = full_length // factor
    folded = signal.reshape(channels, column_count // 2, factor)
    outer_re, outer_im = unit_table(column_count, column_count // 2, column_count, -1.0)
    outer_both = jnp.concatenate([outer_re, outer_im], axis=0)
    first = jnp.einsum("kn,cnm->ckm", outer_both, folded, precision=HIGHEST)
    first_re = first[:, :column_count]
    first_im = first[:, column_count:]
    twist_re, twist_im = unit_table(column_count, factor, full_length, -1.0)
    mid_re = first_re * twist_re - first_im * twist_im
    mid_im = first_re * twist_im + first_im * twist_re
    joined = jnp.concatenate([mid_re, mid_im], axis=2)
    return jnp.einsum("ckn,nm->ckm", joined, block_table(factor, -1.0), precision=HIGHEST)


def inverse(spec_both, factor, length):
    channels = spec_both.shape[0]
    full_length = 2 * length
    column_count = full_length // factor
    mid = jnp.einsum("ckm,mn->ckn", spec_both, block_table(factor, 1.0), precision=HIGHEST)
    mid_re = mid[:, :, :factor]
    mid_im = mid[:, :, factor:]
    twist_re, twist_im = unit_table(column_count, factor, full_length, 1.0)
    turn_re = mid_re * twist_re - mid_im * twist_im
    turn_im = mid_re * twist_im + mid_im * twist_re
    outer_re, outer_im = unit_table(column_count // 2, column_count, column_count, 1.0)
    outer_both = jnp.concatenate([outer_re, -outer_im], axis=1)
    turned = jnp.concatenate([turn_re, turn_im], axis=1)
    result = jnp.einsum("nk,ckm->cnm", outer_both, turned, precision=HIGHEST)
    return result.reshape(channels, length) / full_length


def general_shards(
    gate_input, value_input, short_filter, long_filter, query_weight, key_matrix, value_matrix
):
    seq_rows, local_width = gate_input.shape
    last_rows = gate_input[seq_rows - (TAPS - 1) :]
    earlier = shifted(last_rows, "seq", 1)
    padded = jnp.concatenate([earlier, gate_input], axis=0).astype(jnp.float32)
    kernel = short_filter[:, ::-1].T[:, None, :]
    smoothed = lax.conv_general_dilated(
        padded[None],
        kernel,
        (1,),
        "VALID",
        dimension_numbers=("NHC", "HIO", "NHC"),
        feature_group_count=local_width,
        precision=HIGHEST,
    )[0]
    mixed_input = (smoothed * value_input.astype(jnp.float32)).astype(jnp.bfloat16)
    signal, kernel_line = (
        lax.all_to_all(mixed_input.T, "seq", split_axis=0, concat_axis=1, tiled=True),
        lax.all_to_all(long_filter.T, "seq", split_axis=0, concat_axis=1, tiled=True),
    )
    length = signal.shape[1]
    signal_both = spectrum(signal.astype(jnp.float32), RADIX)
    kernel_both = spectrum(kernel_line.astype(jnp.float32), RADIX)
    signal_re = signal_both[:, :, :RADIX]
    signal_im = signal_both[:, :, RADIX:]
    kernel_re = kernel_both[:, :, :RADIX]
    kernel_im = kernel_both[:, :, RADIX:]
    joint = jnp.concatenate(
        [
            signal_re * kernel_re - signal_im * kernel_im,
            signal_re * kernel_im + signal_im * kernel_re,
        ],
        axis=2,
    )
    conv_line = inverse(joint, RADIX, length).astype(jnp.bfloat16)
    my_index = lax.axis_index("seq")
    group_firsts = [my_index * seq_rows]
    conv_columns = lax.all_to_all(conv_line, "seq", split_axis=1, concat_axis=0, tiled=True)
    heads_here = local_width // HEAD_DIM
    conv_heads = conv_columns.reshape(heads_here, HEAD_DIM, seq_rows)
    query_heads = jnp.einsum(
        "hds,hde->hse", conv_heads, query_weight, preferred_element_type=jnp.float32
    ).astype(jnp.bfloat16)
    group_count = len(group_firsts)
    query_groups = [query_heads]
    key_heads = key_matrix.reshape(seq_rows, heads_here, HEAD_DIM).transpose(1, 0, 2)
    value_heads = value_matrix.reshape(seq_rows, heads_here, HEAD_DIM).transpose(1, 0, 2)
    score_scale = 1.0 / math.sqrt(HEAD_DIM)

    def attend_group(running, group_query, group_first, key_block, value_block, first_row):
        block_rows = key_block.shape[1]

        def compute(current):
            peak_value, weight_sum, weighted = current
            scores = (
                jnp.einsum(
                    "hqd,hkd->hqk", group_query, key_block, preferred_element_type=jnp.float32
                )
                * score_scale
            )
            key_pos = first_row + lax.iota(jnp.int32, block_rows)
            query_pos = group_first + lax.iota(jnp.int32, seq_rows)
            allowed = (key_pos[None, :] <= query_pos[:, None])[None]
            scores = jnp.where(allowed, scores, -1e30)
            new_peak = jnp.maximum(peak_value, jnp.max(scores, axis=2))
            weights = jnp.where(allowed, jnp.exp(scores - new_peak[:, :, None]), 0.0)
            rescale = jnp.exp(peak_value - new_peak)
            weight_sum = weight_sum * rescale + jnp.sum(weights, axis=2)
            weighted = weighted * rescale[:, :, None] + jnp.einsum(
                "hqk,hkd->hqd",
                weights.astype(jnp.bfloat16),
                value_block,
                preferred_element_type=jnp.float32,
            )
            return (new_peak, weight_sum, weighted)

        live = first_row <= group_first + seq_rows - 1
        return lax.cond(live, compute, lambda current: current, running)

    def attend(states, key_block, value_block, first_row):
        return tuple(
            (
                attend_group(
                    states[g], query_groups[g], group_firsts[g], key_block, value_block, first_row
                )
                for g in range(group_count)
            )
        )

    one_state = (
        jnp.full((heads_here, seq_rows), -1e30, jnp.float32),
        jnp.zeros((heads_here, seq_rows), jnp.float32),
        jnp.zeros((heads_here, seq_rows, HEAD_DIM), jnp.float32),
    )
    initial = tuple((one_state for g in range(group_count)))
    running = initial
    key_piece = lax.all_gather(key_heads, "seq", axis=1, tiled=True)
    value_piece = lax.all_gather(value_heads, "seq", axis=1, tiled=True)
    piece_rows = key_piece.shape[1]
    block_rows = 512
    block_count = piece_rows // block_rows
    key_blocks = key_piece.reshape(heads_here, block_count, block_rows, HEAD_DIM).transpose(
        1, 0, 2, 3
    )
    value_blocks = value_piece.reshape(heads_here, block_count, block_rows, HEAD_DIM).transpose(
        1, 0, 2, 3
    )

    def advance(current, element):
        key_block, value_block, position = element
        return (attend(current, key_block, value_block, position * block_rows), None)

    running, _ = lax.scan(
        advance, running, (key_blocks, value_blocks, lax.iota(jnp.int32, block_count))
    )
    outputs = [state[2] / state[1][:, :, None] for state in running]
    result = outputs[0]
    attended_rows = result.transpose(1, 0, 2).reshape(seq_rows, local_width).astype(jnp.bfloat16)
    return attended_rows


def split_pair(array):
    high = array.astype(jnp.bfloat16)
    return high, (array - high.astype(jnp.float32)).astype(jnp.bfloat16)


def transform_tables(rows):
    full = 2 * rows
    turn = np.arange(rows)[:, None] * np.arange(full)[None, :] % full
    angle = 2.0 * np.pi / full * turn
    forward = np.concatenate([np.cos(angle), -np.sin(angle)], axis=0)
    forward[rows] = 1.0 - 2.0 * (np.arange(full) % 2)
    weight = np.full((full,), 2.0 / full)
    weight[0] = weight[rows] = 1.0 / full
    backward = (forward[:, :rows] * weight[:, None]).T
    return forward, backward


def host_split(table):
    high = table.astype(jnp.bfloat16)
    low = (table - high.astype(np.float64)).astype(jnp.bfloat16)
    return jnp.asarray(high), jnp.asarray(low)


def dot(a, b, contract=((1,), (0,))):
    return lax.dot_general(a, b, (contract, ((), ())), preferred_element_type=jnp.float32)


def block_kernel(
    count,
    gate_in,
    value_in,
    long_in,
    key_in,
    val_in,
    short_in,
    weight_in,
    fwd_high_in,
    fwd_low_in,
    inv_high_in,
    inv_low_in,
    out,
    held,
    short_taps,
    head_weight,
    fwd_high,
    fwd_low,
    inv_high,
    inv_low,
    grid_re,
    grid_im,
    grid_nyq,
    sig_re,
    sig_im,
    conv,
    weights,
    sums,
    result,
    send_sem,
    recv_sem,
    own_sem,
    out_send,
    out_recv,
    out_own,
    table_sem,
):
    me = lax.axis_index("seq")
    rows = gate_in.shape[0]
    width = held.shape[2]
    heads = width // HEAD_DIM
    streams = (gate_in, value_in, long_in, key_in, val_in)
    GATE, VALUE, LONG, KEY, VAL = range(5)

    tables = [
        pltpu.make_async_copy(source, target, table_sem.at[i])
        for i, (source, target) in enumerate(
            (
                (fwd_high_in, fwd_high),
                (fwd_low_in, fwd_low),
                (inv_high_in, inv_high),
                (inv_low_in, inv_low),
                (short_in.at[pl.ds(pl.multiple_of(me * width, width), width)], short_taps),
                (weight_in.at[pl.ds(me * heads, heads)], head_weight),
            )
        )
    ]
    for copy in tables:
        copy.start()
    my_rows = pl.ds(pl.multiple_of(me * rows, rows), rows)
    my_columns = pl.ds(pl.multiple_of(me * width, width), width)
    own = [
        pltpu.make_async_copy(stream.at[:, my_columns], held.at[a, my_rows], own_sem.at[a])
        for a, stream in enumerate(streams)
    ]
    for copy in own:
        copy.start()

    barrier = pltpu.get_barrier_semaphore()
    for step in range(1, count):
        peer = lax.rem(me + step, count)
        pl.semaphore_signal(
            barrier, inc=1, device_id={"seq": peer}, device_id_type=pl.DeviceIdType.MESH
        )
    pl.semaphore_wait(barrier, count - 1)

    def exchange(a, step):
        peer = lax.rem(me + step, count)
        peer_columns = pl.ds(pl.multiple_of(peer * width, width), width)
        return pltpu.make_async_remote_copy(
            src_ref=streams[a].at[:, peer_columns],
            dst_ref=held.at[a, my_rows],
            send_sem=send_sem.at[a, peer],
            recv_sem=recv_sem.at[a, me],
            device_id={"seq": peer},
            device_id_type=pl.DeviceIdType.MESH,
        )

    sent = [exchange(a, step) for a in range(5) for step in range(1, count)]
    for copy in sent:
        copy.start()

    def arrive(a):
        own[a].wait()
        for step in range(1, count):
            peer = lax.rem(me + step, count)
            peer_rows = pl.ds(pl.multiple_of(peer * rows, rows), rows)
            pltpu.make_async_remote_copy(
                src_ref=streams[a].at[:, my_columns],
                dst_ref=held.at[a, peer_rows],
                send_sem=send_sem.at[a, peer],
                recv_sem=recv_sem.at[a, peer],
                device_id={"seq": peer},
                device_id_type=pl.DeviceIdType.MESH,
            ).wait_recv()

    for copy in tables:
        copy.wait()

    def forward(signal):
        depth = signal.shape[0]
        both = dot(fwd_high[:, :depth], signal) + dot(fwd_low[:, :depth], signal)
        return both[:rows], both[rows:]

    def backward(re, im):
        re_high, re_low = split_pair(re)
        im_high, im_low = split_pair(im)
        high = jnp.concatenate([re_high, im_high], axis=0)
        low = jnp.concatenate([re_low, im_low], axis=0)
        return dot(inv_high[...], high) + (dot(inv_low[...], high) + dot(inv_high[...], low))

    def factor_parts(re, im):
        first = lax.broadcasted_iota(jnp.int32, re.shape, 0) == 0
        return re, jnp.where(first, 0.0, im), jnp.where(first, im, re)

    def window(a, block):
        now = held[a, block * rows : (block + 1) * rows]
        if block == 0:
            return now
        return jnp.concatenate([now, held[a, (block - 1) * rows : block * rows]], axis=0)

    taps_high, taps_low = split_pair(short_taps[...])
    last = ((1,), (1,))
    taps_both = dot(fwd_high[:, :TAPS], taps_high, last) + (
        dot(fwd_low[:, :TAPS], taps_high, last) + dot(fwd_high[:, :TAPS], taps_low, last)
    )
    taps_re, taps_im, taps_nyq = factor_parts(taps_both[:rows], taps_both[rows:])

    arrive(GATE)
    arrive(VALUE)
    for block in range(count):
        re, im = forward(window(GATE, block))
        smoothed = backward(re * taps_re - im * taps_im, re * taps_im + im * taps_nyq)
        mixed = (
            smoothed * held[VALUE, block * rows : (block + 1) * rows].astype(jnp.float32)
        ).astype(jnp.bfloat16)
        re, im = forward(mixed)
        sig_re[block], sig_im[block] = re, im

    arrive(LONG)
    for block in range(count):
        re, im, nyq = factor_parts(*forward(window(LONG, block)))
        grid_re[block], grid_im[block], grid_nyq[block] = re, im, nyq
    for block in range(count):
        re = im = None
        for source in range(block + 1):
            lag = block - source
            s_re, s_im = sig_re[source], sig_im[source]
            re_term = s_re * grid_re[lag] - s_im * grid_im[lag]
            im_term = s_re * grid_im[lag] + s_im * grid_nyq[lag]
            re = re_term if re is None else re + re_term
            im = im_term if im is None else im + im_term
        conv[block * rows : (block + 1) * rows] = backward(re, im).astype(jnp.bfloat16)

    arrive(KEY)
    scale = 1.0 / math.sqrt(HEAD_DIM)
    for head in range(heads):
        columns = slice(head * HEAD_DIM, (head + 1) * HEAD_DIM)
        for block in range(count):
            here = slice(block * rows, (block + 1) * rows)
            past = (block + 1) * rows
            query = dot(conv[here, columns], head_weight[head]).astype(jnp.bfloat16)
            scores = dot(query, held[KEY, :past, columns], last) * scale
            key_pos = lax.broadcasted_iota(jnp.int32, scores.shape, 1)
            query_pos = block * rows + lax.broadcasted_iota(jnp.int32, scores.shape, 0)
            allowed = key_pos <= query_pos
            scores = jnp.where(allowed, scores, -1e30)
            peak = jnp.max(scores, axis=1, keepdims=True)
            share = jnp.where(allowed, jnp.exp(scores - peak), 0.0)
            sums[head, here] = jnp.broadcast_to(
                jnp.sum(share, axis=1, keepdims=True), (rows, HEAD_DIM)
            )
            weights[head, here, :past] = share.astype(jnp.bfloat16)

    arrive(VAL)

    def give_back(block, head, peer):
        columns = pl.ds(pl.multiple_of(me * width + head * HEAD_DIM, HEAD_DIM), HEAD_DIM)
        return pltpu.make_async_remote_copy(
            src_ref=result.at[head, block * rows : (block + 1) * rows],
            dst_ref=out.at[:, columns],
            send_sem=out_send.at[block, head],
            recv_sem=out_recv.at[me, head],
            device_id={"seq": peer},
            device_id_type=pl.DeviceIdType.MESH,
        )

    def keep(block, head):
        columns = pl.ds(pl.multiple_of(me * width + head * HEAD_DIM, HEAD_DIM), HEAD_DIM)
        return pltpu.make_async_copy(
            result.at[head, block * rows : (block + 1) * rows], out.at[:, columns], out_own.at[head]
        )

    for head in range(heads):
        for block in reversed(range(count)):
            here = slice(block * rows, (block + 1) * rows)
            past = (block + 1) * rows
            columns = slice(head * HEAD_DIM, (head + 1) * HEAD_DIM)
            product = dot(weights[head, here, :past], held[VAL, :past, columns])
            result[head, here] = (product / sums[head, here]).astype(jnp.bfloat16)

            @pl.when(me != block)
            def _():
                give_back(block, head, block).start()

            @pl.when(me == block)
            def _():
                keep(block, head).start()

    for copy in sent:
        copy.wait_send()
    for head in range(heads):
        for step in range(1, count):
            peer = lax.rem(me + step, count)
            columns = pl.ds(pl.multiple_of(peer * width + head * HEAD_DIM, HEAD_DIM), HEAD_DIM)
            pltpu.make_async_remote_copy(
                src_ref=result.at[head, :rows],
                dst_ref=out.at[:, columns],
                send_sem=out_send.at[0, head],
                recv_sem=out_recv.at[peer, head],
                device_id={"seq": peer},
                device_id_type=pl.DeviceIdType.MESH,
            ).wait_recv()
        for block in range(count):

            @pl.when(me != block)
            def _():
                give_back(block, head, block).wait_send()

            @pl.when(me == block)
            def _():
                keep(block, head).wait()


def head_shards(
    count, gate_input, value_input, short_filter, long_filter, query_weight, key_matrix, value_matrix
):
    rows, local_width = gate_input.shape
    width = local_width // count
    heads = width // HEAD_DIM
    length = count * rows
    forward, inverse_table = transform_tables(rows)
    forward = host_split(forward)
    inverse_table = host_split(inverse_table)
    bf16, f32 = jnp.bfloat16, jnp.float32
    return pl.pallas_call(
        functools.partial(block_kernel, count),
        out_shape=jax.ShapeDtypeStruct((rows, local_width), bf16),
        in_specs=[pl.BlockSpec(memory_space=pl.ANY)] * 11,
        out_specs=pl.BlockSpec(memory_space=pl.ANY),
        scratch_shapes=[
            pltpu.VMEM((5, length, width), bf16),
            pltpu.VMEM((width, TAPS), f32),
            pltpu.VMEM((heads, HEAD_DIM, HEAD_DIM), bf16),
            pltpu.VMEM((2 * rows, 2 * rows), bf16),
            pltpu.VMEM((2 * rows, 2 * rows), bf16),
            pltpu.VMEM((rows, 2 * rows), bf16),
            pltpu.VMEM((rows, 2 * rows), bf16),
            pltpu.VMEM((count, rows, width), f32),
            pltpu.VMEM((count, rows, width), f32),
            pltpu.VMEM((count, rows, width), f32),
            pltpu.VMEM((count, rows, width), f32),
            pltpu.VMEM((count, rows, width), f32),
            pltpu.VMEM((length, width), bf16),
            pltpu.VMEM((heads, length, length), bf16),
            pltpu.VMEM((heads, length, HEAD_DIM), f32),
            pltpu.VMEM((heads, length, HEAD_DIM), bf16),
            pltpu.SemaphoreType.DMA((5, count)),
            pltpu.SemaphoreType.DMA((5, count)),
            pltpu.SemaphoreType.DMA((5,)),
            pltpu.SemaphoreType.DMA((count, heads)),
            pltpu.SemaphoreType.DMA((count, heads)),
            pltpu.SemaphoreType.DMA((heads,)),
            pltpu.SemaphoreType.DMA((6,)),
        ],
        compiler_params=pltpu.CompilerParams(collective_id=0, has_side_effects=True),
    )(
        gate_input,
        value_input,
        long_filter,
        key_matrix,
        value_matrix,
        short_filter,
        query_weight,
        *forward,
        *inverse_table,
    )


def shards(count, gate_input, *others):
    rows, local_width = gate_input.shape
    by_heads = local_width % (count * HEAD_DIM) == 0 and rows >= TAPS and rows % HEAD_DIM == 0
    if count > 1 and by_heads:
        return head_shards(count, gate_input, *others)
    return general_shards(gate_input, *others)


def solution(mesh):
    in_specs = (
        P(("groups", "seq"), "chan"),
        P(("groups", "seq"), "chan"),
        P("chan", None),
        P("seq", "chan"),
        P("chan", None, None),
        P(("groups", "seq"), "chan"),
        P(("groups", "seq"), "chan"),
    )
    out_specs = P(("groups", "seq"), "chan")
    return jax.shard_map(
        functools.partial(shards, mesh.shape["seq"]), mesh=mesh, in_specs=in_specs, out_specs=out_specs, check_vma=False)
```

```python
import functools
import math

import jax
import jax.numpy as jnp
import numpy as np
from jax import lax
from jax.experimental import pallas as pl
from jax.experimental.pallas import tpu as pltpu
from jax.sharding import PartitionSpec as P

HEAD_DIM = 128
TAPS = 128
RADIX = 128


HIGHEST = lax.Precision.HIGHEST


def shifted(value, axis, steps):
    count = lax.axis_size(axis)
    initial, last = (max(0, -steps), min(count, count - steps))
    return lax.ppermute(value, axis, [(source, source + steps) for source in range(initial, last)])


def unit_table(height, breadth, modulus, orient):
    product = (
        lax.broadcasted_iota(jnp.int32, (height, breadth), 0)
        * lax.broadcasted_iota(jnp.int32, (height, breadth), 1)
        % modulus
    )
    angles = 2.0 * math.pi / modulus * product.astype(jnp.float32)
    return (jnp.cos(angles), orient * jnp.sin(angles))


def block_table(factor, orient):
    inner_re, inner_im = unit_table(factor, factor, factor, orient)
    upper = jnp.concatenate([inner_re, inner_im], axis=1)
    lower = jnp.concatenate([-inner_im, inner_re], axis=1)
    return jnp.concatenate([upper, lower], axis=0)


def spectrum(signal, factor):
    channels, length = signal.shape
    full_length = 2 * length
    column_count = full_length // factor
    folded = signal.reshape(channels, column_count // 2, factor)
    outer_re, outer_im = unit_table(column_count, column_count // 2, column_count, -1.0)
    outer_both = jnp.concatenate([outer_re, outer_im], axis=0)
    first = jnp.einsum("kn,cnm->ckm", outer_both, folded, precision=HIGHEST)
    first_re = first[:, :column_count]
    first_im = first[:, column_count:]
    twist_re, twist_im = unit_table(column_count, factor, full_length, -1.0)
    mid_re = first_re * twist_re - first_im * twist_im
    mid_im = first_re * twist_im + first_im * twist_re
    joined = jnp.concatenate([mid_re, mid_im], axis=2)
    return jnp.einsum("ckn,nm->ckm", joined, block_table(factor, -1.0), precision=HIGHEST)


def inverse(spec_both, factor, length):
    channels = spec_both.shape[0]
    full_length = 2 * length
    column_count = full_length // factor
    mid = jnp.einsum("ckm,mn->ckn", spec_both, block_table(factor, 1.0), precision=HIGHEST)
    mid_re = mid[:, :, :factor]
    mid_im = mid[:, :, factor:]
    twist_re, twist_im = unit_table(column_count, factor, full_length, 1.0)
    turn_re = mid_re * twist_re - mid_im * twist_im
    turn_im = mid_re * twist_im + mid_im * twist_re
    outer_re, outer_im = unit_table(column_count // 2, column_count, column_count, 1.0)
    outer_both = jnp.concatenate([outer_re, -outer_im], axis=1)
    turned = jnp.concatenate([turn_re, turn_im], axis=1)
    result = jnp.einsum("nk,ckm->cnm", outer_both, turned, precision=HIGHEST)
    return result.reshape(channels, length) / full_length


def general_shards(
    gate_input, value_input, short_filter, long_filter, query_weight, key_matrix, value_matrix
):
    seq_rows, local_width = gate_input.shape
    last_rows = gate_input[seq_rows - (TAPS - 1) :]
    earlier = shifted(last_rows, "seq", 1)
    padded = jnp.concatenate([earlier, gate_input], axis=0).astype(jnp.float32)
    kernel = short_filter[:, ::-1].T[:, None, :]
    smoothed = lax.conv_general_dilated(
        padded[None],
        kernel,
        (1,),
        "VALID",
        dimension_numbers=("NHC", "HIO", "NHC"),
        feature_group_count=local_width,
        precision=HIGHEST,
    )[0]
    mixed_input = (smoothed * value_input.astype(jnp.float32)).astype(jnp.bfloat16)
    signal, kernel_line = (
        lax.all_to_all(mixed_input.T, "seq", split_axis=0, concat_axis=1, tiled=True),
        lax.all_to_all(long_filter.T, "seq", split_axis=0, concat_axis=1, tiled=True),
    )
    length = signal.shape[1]
    signal_both = spectrum(signal.astype(jnp.float32), RADIX)
    kernel_both = spectrum(kernel_line.astype(jnp.float32), RADIX)
    signal_re = signal_both[:, :, :RADIX]
    signal_im = signal_both[:, :, RADIX:]
    kernel_re = kernel_both[:, :, :RADIX]
    kernel_im = kernel_both[:, :, RADIX:]
    joint = jnp.concatenate(
        [
            signal_re * kernel_re - signal_im * kernel_im,
            signal_re * kernel_im + signal_im * kernel_re,
        ],
        axis=2,
    )
    conv_line = inverse(joint, RADIX, length).astype(jnp.bfloat16)
    my_index = lax.axis_index("seq")
    group_firsts = [my_index * seq_rows]
    conv_columns = lax.all_to_all(conv_line, "seq", split_axis=1, concat_axis=0, tiled=True)
    heads_here = local_width // HEAD_DIM
    conv_heads = conv_columns.reshape(heads_here, HEAD_DIM, seq_rows)
    query_heads = jnp.einsum(
        "hds,hde->hse", conv_heads, query_weight, preferred_element_type=jnp.float32
    ).astype(jnp.bfloat16)
    group_count = len(group_firsts)
    query_groups = [query_heads]
    key_heads = key_matrix.reshape(seq_rows, heads_here, HEAD_DIM).transpose(1, 0, 2)
    value_heads = value_matrix.reshape(seq_rows, heads_here, HEAD_DIM).transpose(1, 0, 2)
    score_scale = 1.0 / math.sqrt(HEAD_DIM)

    def attend_group(running, group_query, group_first, key_block, value_block, first_row):
        block_rows = key_block.shape[1]

        def compute(current):
            peak_value, weight_sum, weighted = current
            scores = (
                jnp.einsum(
                    "hqd,hkd->hqk", group_query, key_block, preferred_element_type=jnp.float32
                )
                * score_scale
            )
            key_pos = first_row + lax.iota(jnp.int32, block_rows)
            query_pos = group_first + lax.iota(jnp.int32, seq_rows)
            allowed = (key_pos[None, :] <= query_pos[:, None])[None]
            scores = jnp.where(allowed, scores, -1e30)
            new_peak = jnp.maximum(peak_value, jnp.max(scores, axis=2))
            weights = jnp.where(allowed, jnp.exp(scores - new_peak[:, :, None]), 0.0)
            rescale = jnp.exp(peak_value - new_peak)
            weight_sum = weight_sum * rescale + jnp.sum(weights, axis=2)
            weighted = weighted * rescale[:, :, None] + jnp.einsum(
                "hqk,hkd->hqd",
                weights.astype(jnp.bfloat16),
                value_block,
                preferred_element_type=jnp.float32,
            )
            return (new_peak, weight_sum, weighted)

        live = first_row <= group_first + seq_rows - 1
        return lax.cond(live, compute, lambda current: current, running)

    def attend(states, key_block, value_block, first_row):
        return tuple(
            (
                attend_group(
                    states[g], query_groups[g], group_firsts[g], key_block, value_block, first_row
                )
                for g in range(group_count)
            )
        )

    one_state = (
        jnp.full((heads_here, seq_rows), -1e30, jnp.float32),
        jnp.zeros((heads_here, seq_rows), jnp.float32),
        jnp.zeros((heads_here, seq_rows, HEAD_DIM), jnp.float32),
    )
    initial = tuple((one_state for g in range(group_count)))
    running = initial
    key_piece = lax.all_gather(key_heads, "seq", axis=1, tiled=True)
    value_piece = lax.all_gather(value_heads, "seq", axis=1, tiled=True)
    piece_rows = key_piece.shape[1]
    block_rows = 512
    block_count = piece_rows // block_rows
    key_blocks = key_piece.reshape(heads_here, block_count, block_rows, HEAD_DIM).transpose(
        1, 0, 2, 3
    )
    value_blocks = value_piece.reshape(heads_here, block_count, block_rows, HEAD_DIM).transpose(
        1, 0, 2, 3
    )

    def advance(current, element):
        key_block, value_block, position = element
        return (attend(current, key_block, value_block, position * block_rows), None)

    running, _ = lax.scan(
        advance, running, (key_blocks, value_blocks, lax.iota(jnp.int32, block_count))
    )
    outputs = [state[2] / state[1][:, :, None] for state in running]
    result = outputs[0]
    attended_rows = result.transpose(1, 0, 2).reshape(seq_rows, local_width).astype(jnp.bfloat16)
    return attended_rows


def split_pair(array):
    high = array.astype(jnp.bfloat16)
    return high, (array - high.astype(jnp.float32)).astype(jnp.bfloat16)


def transform_tables(rows):
    full = 2 * rows
    turn = np.arange(rows)[:, None] * np.arange(full)[None, :] % full
    angle = 2.0 * np.pi / full * turn
    forward = np.concatenate([np.cos(angle), -np.sin(angle)], axis=0)
    forward[rows] = 1.0 - 2.0 * (np.arange(full) % 2)
    weight = np.full((full,), 2.0 / full)
    weight[0] = weight[rows] = 1.0 / full
    backward = (forward[:, :rows] * weight[:, None]).T
    return forward, backward


def host_split(table):
    high = table.astype(jnp.bfloat16)
    low = (table - high.astype(np.float64)).astype(jnp.bfloat16)
    return jnp.asarray(high), jnp.asarray(low)


def dot(a, b, contract=((1,), (0,))):
    return lax.dot_general(a, b, (contract, ((), ())), preferred_element_type=jnp.float32)


def block_kernel(
    count,
    gate_in,
    value_in,
    long_in,
    key_in,
    val_in,
    short_in,
    weight_in,
    fwd_high_in,
    fwd_low_in,
    inv_high_in,
    inv_low_in,
    out,
    held,
    short_taps,
    head_weight,
    fwd_high,
    fwd_low,
    inv_high,
    inv_low,
    grid_re,
    grid_im,
    grid_nyq,
    sig_re,
    sig_im,
    conv,
    weights,
    sums,
    result,
    smoothed,
    pass_send,
    pass_recv,
    send_sem,
    recv_sem,
    own_sem,
    out_send,
    out_recv,
    out_own,
    table_sem,
):
    me = lax.axis_index("seq")
    rows = gate_in.shape[0]
    width = held.shape[2]
    heads = width // HEAD_DIM
    streams = (gate_in, value_in, long_in, key_in, val_in)
    GATE, VALUE, LONG, KEY, VAL = range(5)
    groups = lax.axis_size("groups")
    my_group = lax.axis_index("groups")
    share = width // groups

    def flip(index):
        return index + 1 - 2 * lax.rem(index, 2)

    partner = flip(me)
    far = []
    for step in range(2, count, 2):
        other = lax.rem(me + step, count)
        far += [other, flip(other)]
    peers = [*far, partner]

    tables = [
        pltpu.make_async_copy(source, target, table_sem.at[i])
        for i, (source, target) in enumerate(
            (
                (fwd_high_in, fwd_high),
                (fwd_low_in, fwd_low),
                (inv_high_in, inv_high),
                (inv_low_in, inv_low),
                (short_in.at[pl.ds(pl.multiple_of(me * width, width), width)], short_taps),
                (weight_in.at[pl.ds(me * heads, heads)], head_weight),
            )
        )
    ]
    for copy in tables:
        copy.start()
    my_rows = pl.ds(pl.multiple_of(me * rows, rows), rows)
    my_columns = pl.ds(pl.multiple_of(me * width, width), width)
    own = [
        pltpu.make_async_copy(stream.at[:, my_columns], held.at[a, my_rows], own_sem.at[a])
        for a, stream in enumerate(streams)
    ]
    for copy in own:
        copy.start()

    barrier = pltpu.get_barrier_semaphore()
    siblings = [lax.rem(my_group + step, groups) for step in range(1, groups)]
    for peer in peers:
        pl.semaphore_signal(
            barrier, inc=1, device_id={"seq": peer}, device_id_type=pl.DeviceIdType.MESH
        )
    for sibling in siblings:
        pl.semaphore_signal(
            barrier, inc=1, device_id={"groups": sibling}, device_id_type=pl.DeviceIdType.MESH
        )
    pl.semaphore_wait(barrier, len(peers) + len(siblings))

    def block_of(index):
        return pl.ds(pl.multiple_of(index * rows, rows), rows)

    def exchange(a, slot, peer, source, first, breadth):
        there = pl.ds(pl.multiple_of(peer * width + first, HEAD_DIM), breadth)
        here = pl.ds(pl.multiple_of(first, HEAD_DIM), breadth)
        return pltpu.make_async_remote_copy(
            src_ref=streams[a].at[:, there],
            dst_ref=held.at[a, block_of(source), here],
            send_sem=send_sem.at[slot, peer],
            recv_sem=recv_sem.at[slot, source],
            device_id={"seq": peer},
            device_id_type=pl.DeviceIdType.MESH,
        )

    def pass_on(step, source):
        here = pl.ds(pl.multiple_of(my_group * share, HEAD_DIM), share)
        return pltpu.make_async_remote_copy(
            src_ref=held.at[LONG, block_of(source), here],
            dst_ref=held.at[LONG, block_of(source), here],
            send_sem=pass_send.at[step, source],
            recv_sem=pass_recv.at[step, source],
            device_id={"groups": siblings[step]},
            device_id_type=pl.DeviceIdType.MESH,
        )

    def long_part(peer):
        return (0, width) if peer is partner else (my_group * share, share)

    sent = []
    for peer in peers:
        sent.append(exchange(LONG, 0, peer, me, *long_part(peer)))
    for a, slot in ((GATE, 1), (VALUE, 2)):
        for peer in peers:
            sent.append(exchange(a, slot, peer, me, 0, width))
    for head in range(heads):
        for a, slot in ((KEY, 3 + 2 * head), (VAL, 4 + 2 * head)):
            for peer in peers:
                sent.append(exchange(a, slot, peer, me, head * HEAD_DIM, HEAD_DIM))
    for copy in sent:
        copy.start()

    def arrive(a, slot, first=0, breadth=width):
        for peer in peers:
            exchange(a, slot, peer, peer, first, breadth).wait_recv()

    for copy in tables:
        copy.wait()

    def forward(signal):
        depth = signal.shape[0]
        both = dot(fwd_high[:, :depth], signal) + dot(fwd_low[:, :depth], signal)
        return both[:rows], both[rows:]

    def backward(re, im):
        re_high, re_low = split_pair(re)
        im_high, im_low = split_pair(im)
        high = jnp.concatenate([re_high, im_high], axis=0)
        low = jnp.concatenate([re_low, im_low], axis=0)
        return dot(inv_high[...], high) + (dot(inv_low[...], high) + dot(inv_high[...], low))

    def factor_parts(re, im):
        first = lax.broadcasted_iota(jnp.int32, re.shape, 0) == 0
        return re, jnp.where(first, 0.0, im), jnp.where(first, im, re)

    def window(a, block):
        now = held[a, block * rows : (block + 1) * rows]
        if block == 0:
            return now
        return jnp.concatenate([now, held[a, (block - 1) * rows : block * rows]], axis=0)

    taps_high, taps_low = split_pair(short_taps[...])
    last = ((1,), (1,))
    taps_both = dot(fwd_high[:, :TAPS], taps_high, last) + (
        dot(fwd_low[:, :TAPS], taps_high, last) + dot(fwd_high[:, :TAPS], taps_low, last)
    )
    taps_re, taps_im, taps_nyq = factor_parts(taps_both[:rows], taps_both[rows:])

    passed = []
    for peer in peers:
        exchange(LONG, 0, peer, peer, *long_part(peer)).wait_recv()
        if peer is not partner:
            for step in range(groups - 1):
                passed.append(pass_on(step, peer))
                passed[-1].start()

    own[GATE].wait()
    arrive(GATE, 1)
    for block in range(count):
        re, im = forward(window(GATE, block))
        smoothed[block] = backward(re * taps_re - im * taps_im, re * taps_im + im * taps_nyq)

    own[LONG].wait()
    for copy in passed:
        copy.wait_recv()
    for block in range(count):
        re, im, nyq = factor_parts(*forward(window(LONG, block)))
        grid_re[block], grid_im[block], grid_nyq[block] = re, im, nyq

    own[VALUE].wait()
    arrive(VALUE, 2)
    for block in range(count):
        here = slice(block * rows, (block + 1) * rows)
        mixed = (smoothed[block] * held[VALUE, here].astype(jnp.float32)).astype(jnp.bfloat16)
        sig_re[block], sig_im[block] = forward(mixed)

    for block in range(count):
        re = im = None
        for source in range(block + 1):
            lag = block - source
            s_re, s_im = sig_re[source], sig_im[source]
            re_term = s_re * grid_re[lag] - s_im * grid_im[lag]
            im_term = s_re * grid_im[lag] + s_im * grid_nyq[lag]
            re = re_term if re is None else re + re_term
            im = im_term if im is None else im + im_term
        conv[block * rows : (block + 1) * rows] = backward(re, im).astype(jnp.bfloat16)

    def give_back(block, head, peer):
        columns = pl.ds(pl.multiple_of(me * width + head * HEAD_DIM, HEAD_DIM), HEAD_DIM)
        return pltpu.make_async_remote_copy(
            src_ref=result.at[head, block * rows : (block + 1) * rows],
            dst_ref=out.at[:, columns],
            send_sem=out_send.at[block, head],
            recv_sem=out_recv.at[me, head],
            device_id={"seq": peer},
            device_id_type=pl.DeviceIdType.MESH,
        )

    def keep(block, head):
        columns = pl.ds(pl.multiple_of(me * width + head * HEAD_DIM, HEAD_DIM), HEAD_DIM)
        return pltpu.make_async_copy(
            result.at[head, block * rows : (block + 1) * rows], out.at[:, columns], out_own.at[head]
        )

    scale = 1.0 / math.sqrt(HEAD_DIM)
    own[KEY].wait()
    own[VAL].wait()
    for head in range(heads):
        arrive(KEY, 3 + 2 * head, head * HEAD_DIM, HEAD_DIM)
        columns = slice(head * HEAD_DIM, (head + 1) * HEAD_DIM)
        for block in range(count):
            here = slice(block * rows, (block + 1) * rows)
            past = (block + 1) * rows
            query = dot(conv[here, columns], head_weight[head]).astype(jnp.bfloat16)
            scores = dot(query, held[KEY, :past, columns], last) * scale
            key_pos = lax.broadcasted_iota(jnp.int32, scores.shape, 1)
            query_pos = block * rows + lax.broadcasted_iota(jnp.int32, scores.shape, 0)
            allowed = key_pos <= query_pos
            scores = jnp.where(allowed, scores, -1e30)
            peak = jnp.max(scores, axis=1, keepdims=True)
            share = jnp.where(allowed, jnp.exp(scores - peak), 0.0)
            sums[head, here] = jnp.broadcast_to(
                jnp.sum(share, axis=1, keepdims=True), (rows, HEAD_DIM)
            )
            weights[head, here, :past] = share.astype(jnp.bfloat16)

        arrive(VAL, 4 + 2 * head, head * HEAD_DIM, HEAD_DIM)
        for block in reversed(range(count)):
            here = slice(block * rows, (block + 1) * rows)
            past = (block + 1) * rows
            columns = slice(head * HEAD_DIM, (head + 1) * HEAD_DIM)
            product = dot(weights[head, here, :past], held[VAL, :past, columns])
            result[head, here] = (product / sums[head, here]).astype(jnp.bfloat16)

            @pl.when(me != block)
            def _():
                give_back(block, head, block).start()

            @pl.when(me == block)
            def _():
                keep(block, head).start()

    for copy in [*sent, *passed]:
        copy.wait_send()
    for head in range(heads):
        for peer in peers:
            columns = pl.ds(pl.multiple_of(peer * width + head * HEAD_DIM, HEAD_DIM), HEAD_DIM)
            pltpu.make_async_remote_copy(
                src_ref=result.at[head, :rows],
                dst_ref=out.at[:, columns],
                send_sem=out_send.at[0, head],
                recv_sem=out_recv.at[peer, head],
                device_id={"seq": peer},
                device_id_type=pl.DeviceIdType.MESH,
            ).wait_recv()
        for block in range(count):

            @pl.when(me != block)
            def _():
                give_back(block, head, block).wait_send()

            @pl.when(me == block)
            def _():
                keep(block, head).wait()


def head_shards(
    count,
    groups,
    gate_input,
    value_input,
    short_filter,
    long_filter,
    query_weight,
    key_matrix,
    value_matrix,
):
    rows, local_width = gate_input.shape
    width = local_width // count
    heads = width // HEAD_DIM
    length = count * rows
    forward, inverse_table = transform_tables(rows)
    forward = host_split(forward)
    inverse_table = host_split(inverse_table)
    bf16, f32 = jnp.bfloat16, jnp.float32
    return pl.pallas_call(
        functools.partial(block_kernel, count),
        out_shape=pltpu.VMEM((rows, local_width), bf16),
        in_specs=[pl.BlockSpec(memory_space=pl.ANY)] * 11,
        out_specs=pl.BlockSpec(memory_space=pltpu.VMEM),
        scratch_shapes=[
            pltpu.VMEM((5, length, width), bf16),
            pltpu.VMEM((width, TAPS), f32),
            pltpu.VMEM((heads, HEAD_DIM, HEAD_DIM), bf16),
            pltpu.VMEM((2 * rows, 2 * rows), bf16),
            pltpu.VMEM((2 * rows, 2 * rows), bf16),
            pltpu.VMEM((rows, 2 * rows), bf16),
            pltpu.VMEM((rows, 2 * rows), bf16),
            pltpu.VMEM((count, rows, width), f32),
            pltpu.VMEM((count, rows, width), f32),
            pltpu.VMEM((count, rows, width), f32),
            pltpu.VMEM((count, rows, width), f32),
            pltpu.VMEM((count, rows, width), f32),
            pltpu.VMEM((length, width), bf16),
            pltpu.VMEM((heads, length, length), bf16),
            pltpu.VMEM((heads, length, HEAD_DIM), f32),
            pltpu.VMEM((heads, length, HEAD_DIM), bf16),
            pltpu.VMEM((count, rows, width), f32),
            pltpu.SemaphoreType.DMA((groups - 1, count)),
            pltpu.SemaphoreType.DMA((groups - 1, count)),
            pltpu.SemaphoreType.DMA((3 + 2 * heads, count)),
            pltpu.SemaphoreType.DMA((3 + 2 * heads, count)),
            pltpu.SemaphoreType.DMA((5,)),
            pltpu.SemaphoreType.DMA((count, heads)),
            pltpu.SemaphoreType.DMA((count, heads)),
            pltpu.SemaphoreType.DMA((heads,)),
            pltpu.SemaphoreType.DMA((6,)),
        ],
        compiler_params=pltpu.CompilerParams(collective_id=0, has_side_effects=True),
    )(
        gate_input,
        value_input,
        long_filter,
        key_matrix,
        value_matrix,
        short_filter,
        query_weight,
        *forward,
        *inverse_table,
    )


def shards(count, groups, gate_input, *others):
    rows, local_width = gate_input.shape
    by_heads = local_width % (count * groups * HEAD_DIM) == 0
    by_rows = rows >= TAPS and rows % HEAD_DIM == 0
    if count % 2 == 0 and groups > 1 and by_heads and by_rows:
        return head_shards(count, groups, gate_input, *others)
    return general_shards(gate_input, *others)


def solution(mesh):
    in_specs = (
        P(("groups", "seq"), "chan"),
        P(("groups", "seq"), "chan"),
        P("chan", None),
        P("seq", "chan"),
        P("chan", None, None),
        P(("groups", "seq"), "chan"),
        P(("groups", "seq"), "chan"),
    )
    out_specs = P(("groups", "seq"), "chan")
    return jax.shard_map(
        functools.partial(shards, mesh.shape["seq"], mesh.shape["groups"]), mesh=mesh, in_specs=in_specs, out_specs=out_specs, check_vma=False)
```

```python
import functools
import math

import jax
import jax.numpy as jnp
import numpy as np
from jax import lax
from jax.experimental import pallas as pl
from jax.experimental.pallas import tpu as pltpu
from jax.sharding import PartitionSpec as P

HEAD_DIM = 128
TAPS = 128
RADIX = 128


HIGHEST = lax.Precision.HIGHEST


def shifted(value, axis, steps):
    count = lax.axis_size(axis)
    initial, last = (max(0, -steps), min(count, count - steps))
    return lax.ppermute(value, axis, [(source, source + steps) for source in range(initial, last)])


def unit_table(height, breadth, modulus, orient):
    product = (
        lax.broadcasted_iota(jnp.int32, (height, breadth), 0)
        * lax.broadcasted_iota(jnp.int32, (height, breadth), 1)
        % modulus
    )
    angles = 2.0 * math.pi / modulus * product.astype(jnp.float32)
    return (jnp.cos(angles), orient * jnp.sin(angles))


def block_table(factor, orient):
    inner_re, inner_im = unit_table(factor, factor, factor, orient)
    upper = jnp.concatenate([inner_re, inner_im], axis=1)
    lower = jnp.concatenate([-inner_im, inner_re], axis=1)
    return jnp.concatenate([upper, lower], axis=0)


def spectrum(signal, factor):
    channels, length = signal.shape
    full_length = 2 * length
    column_count = full_length // factor
    folded = signal.reshape(channels, column_count // 2, factor)
    outer_re, outer_im = unit_table(column_count, column_count // 2, column_count, -1.0)
    outer_both = jnp.concatenate([outer_re, outer_im], axis=0)
    first = jnp.einsum("kn,cnm->ckm", outer_both, folded, precision=HIGHEST)
    first_re = first[:, :column_count]
    first_im = first[:, column_count:]
    twist_re, twist_im = unit_table(column_count, factor, full_length, -1.0)
    mid_re = first_re * twist_re - first_im * twist_im
    mid_im = first_re * twist_im + first_im * twist_re
    joined = jnp.concatenate([mid_re, mid_im], axis=2)
    return jnp.einsum("ckn,nm->ckm", joined, block_table(factor, -1.0), precision=HIGHEST)


def inverse(spec_both, factor, length):
    channels = spec_both.shape[0]
    full_length = 2 * length
    column_count = full_length // factor
    mid = jnp.einsum("ckm,mn->ckn", spec_both, block_table(factor, 1.0), precision=HIGHEST)
    mid_re = mid[:, :, :factor]
    mid_im = mid[:, :, factor:]
    twist_re, twist_im = unit_table(column_count, factor, full_length, 1.0)
    turn_re = mid_re * twist_re - mid_im * twist_im
    turn_im = mid_re * twist_im + mid_im * twist_re
    outer_re, outer_im = unit_table(column_count // 2, column_count, column_count, 1.0)
    outer_both = jnp.concatenate([outer_re, -outer_im], axis=1)
    turned = jnp.concatenate([turn_re, turn_im], axis=1)
    result = jnp.einsum("nk,ckm->cnm", outer_both, turned, precision=HIGHEST)
    return result.reshape(channels, length) / full_length


def general_shards(
    gate_input, value_input, short_filter, long_filter, query_weight, key_matrix, value_matrix
):
    seq_rows, local_width = gate_input.shape
    last_rows = gate_input[seq_rows - (TAPS - 1) :]
    earlier = shifted(last_rows, "seq", 1)
    padded = jnp.concatenate([earlier, gate_input], axis=0).astype(jnp.float32)
    kernel = short_filter[:, ::-1].T[:, None, :]
    smoothed = lax.conv_general_dilated(
        padded[None],
        kernel,
        (1,),
        "VALID",
        dimension_numbers=("NHC", "HIO", "NHC"),
        feature_group_count=local_width,
        precision=HIGHEST,
    )[0]
    mixed_input = (smoothed * value_input.astype(jnp.float32)).astype(jnp.bfloat16)
    signal, kernel_line = (
        lax.all_to_all(mixed_input.T, "seq", split_axis=0, concat_axis=1, tiled=True),
        lax.all_to_all(long_filter.T, "seq", split_axis=0, concat_axis=1, tiled=True),
    )
    length = signal.shape[1]
    signal_both = spectrum(signal.astype(jnp.float32), RADIX)
    kernel_both = spectrum(kernel_line.astype(jnp.float32), RADIX)
    signal_re = signal_both[:, :, :RADIX]
    signal_im = signal_both[:, :, RADIX:]
    kernel_re = kernel_both[:, :, :RADIX]
    kernel_im = kernel_both[:, :, RADIX:]
    joint = jnp.concatenate(
        [
            signal_re * kernel_re - signal_im * kernel_im,
            signal_re * kernel_im + signal_im * kernel_re,
        ],
        axis=2,
    )
    conv_line = inverse(joint, RADIX, length).astype(jnp.bfloat16)
    my_index = lax.axis_index("seq")
    group_firsts = [my_index * seq_rows]
    conv_columns = lax.all_to_all(conv_line, "seq", split_axis=1, concat_axis=0, tiled=True)
    heads_here = local_width // HEAD_DIM
    conv_heads = conv_columns.reshape(heads_here, HEAD_DIM, seq_rows)
    query_heads = jnp.einsum(
        "hds,hde->hse", conv_heads, query_weight, preferred_element_type=jnp.float32
    ).astype(jnp.bfloat16)
    group_count = len(group_firsts)
    query_groups = [query_heads]
    key_heads = key_matrix.reshape(seq_rows, heads_here, HEAD_DIM).transpose(1, 0, 2)
    value_heads = value_matrix.reshape(seq_rows, heads_here, HEAD_DIM).transpose(1, 0, 2)
    score_scale = 1.0 / math.sqrt(HEAD_DIM)

    def attend_group(running, group_query, group_first, key_block, value_block, first_row):
        block_rows = key_block.shape[1]

        def compute(current):
            peak_value, weight_sum, weighted = current
            scores = (
                jnp.einsum(
                    "hqd,hkd->hqk", group_query, key_block, preferred_element_type=jnp.float32
                )
                * score_scale
            )
            key_pos = first_row + lax.iota(jnp.int32, block_rows)
            query_pos = group_first + lax.iota(jnp.int32, seq_rows)
            allowed = (key_pos[None, :] <= query_pos[:, None])[None]
            scores = jnp.where(allowed, scores, -1e30)
            new_peak = jnp.maximum(peak_value, jnp.max(scores, axis=2))
            weights = jnp.where(allowed, jnp.exp(scores - new_peak[:, :, None]), 0.0)
            rescale = jnp.exp(peak_value - new_peak)
            weight_sum = weight_sum * rescale + jnp.sum(weights, axis=2)
            weighted = weighted * rescale[:, :, None] + jnp.einsum(
                "hqk,hkd->hqd",
                weights.astype(jnp.bfloat16),
                value_block,
                preferred_element_type=jnp.float32,
            )
            return (new_peak, weight_sum, weighted)

        live = first_row <= group_first + seq_rows - 1
        return lax.cond(live, compute, lambda current: current, running)

    def attend(states, key_block, value_block, first_row):
        return tuple(
            (
                attend_group(
                    states[g], query_groups[g], group_firsts[g], key_block, value_block, first_row
                )
                for g in range(group_count)
            )
        )

    one_state = (
        jnp.full((heads_here, seq_rows), -1e30, jnp.float32),
        jnp.zeros((heads_here, seq_rows), jnp.float32),
        jnp.zeros((heads_here, seq_rows, HEAD_DIM), jnp.float32),
    )
    initial = tuple((one_state for g in range(group_count)))
    running = initial
    key_piece = lax.all_gather(key_heads, "seq", axis=1, tiled=True)
    value_piece = lax.all_gather(value_heads, "seq", axis=1, tiled=True)
    piece_rows = key_piece.shape[1]
    block_rows = 512
    block_count = piece_rows // block_rows
    key_blocks = key_piece.reshape(heads_here, block_count, block_rows, HEAD_DIM).transpose(
        1, 0, 2, 3
    )
    value_blocks = value_piece.reshape(heads_here, block_count, block_rows, HEAD_DIM).transpose(
        1, 0, 2, 3
    )

    def advance(current, element):
        key_block, value_block, position = element
        return (attend(current, key_block, value_block, position * block_rows), None)

    running, _ = lax.scan(
        advance, running, (key_blocks, value_blocks, lax.iota(jnp.int32, block_count))
    )
    outputs = [state[2] / state[1][:, :, None] for state in running]
    result = outputs[0]
    attended_rows = result.transpose(1, 0, 2).reshape(seq_rows, local_width).astype(jnp.bfloat16)
    return attended_rows


def split_pair(array):
    high = array.astype(jnp.bfloat16)
    return high, (array - high.astype(jnp.float32)).astype(jnp.bfloat16)


def transform_tables(rows):
    full = 2 * rows
    turn = np.arange(rows)[:, None] * np.arange(full)[None, :] % full
    angle = 2.0 * np.pi / full * turn
    forward = np.concatenate([np.cos(angle), -np.sin(angle)], axis=0)
    forward[rows] = 1.0 - 2.0 * (np.arange(full) % 2)
    weight = np.full((full,), 2.0 / full)
    weight[0] = weight[rows] = 1.0 / full
    backward = (forward[:, :rows] * weight[:, None]).T
    return forward, backward


def host_split(table):
    high = table.astype(jnp.bfloat16)
    low = (table - high.astype(np.float64)).astype(jnp.bfloat16)
    return jnp.asarray(high), jnp.asarray(low)


def dot(a, b, contract=((1,), (0,))):
    return lax.dot_general(a, b, (contract, ((), ())), preferred_element_type=jnp.float32)


def block_kernel(
    count,
    gate_in,
    value_in,
    long_in,
    key_in,
    val_in,
    short_in,
    weight_in,
    fwd_high_in,
    fwd_low_in,
    inv_high_in,
    inv_low_in,
    out,
    held,
    short_taps,
    head_weight,
    fwd_high,
    fwd_low,
    inv_high,
    inv_low,
    grid_re,
    grid_im,
    grid_nyq,
    sig_re,
    sig_im,
    conv,
    weights,
    sums,
    result,
    smoothed,
    mixed,
    far_taps,
    far_gate,
    far_before,
    far_value,
    far_mixed,
    halo_sem,
    pass_send,
    pass_recv,
    send_sem,
    recv_sem,
    own_sem,
    out_send,
    out_recv,
    out_own,
    table_sem,
):
    me = lax.axis_index("seq")
    rows = gate_in.shape[0]
    width = held.shape[2]
    heads = width // HEAD_DIM
    streams = (gate_in, value_in, long_in, key_in, val_in)
    GATE, VALUE, LONG, KEY, VAL = range(5)
    groups = lax.axis_size("groups")
    my_group = lax.axis_index("groups")
    share = width // groups

    def flip(index):
        return index + 1 - 2 * lax.rem(index, 2)

    partner = flip(me)
    opposite = lax.rem(me + 2, count)
    far = [opposite, flip(opposite)]
    peers = [*far, partner]
    late = me // 2
    far_columns = pl.ds(pl.multiple_of((1 - late) * 2 * width, 2 * width), 2 * width)

    tables = [
        pltpu.make_async_copy(source, target, table_sem.at[i])
        for i, (source, target) in enumerate(
            (
                (fwd_high_in, fwd_high),
                (fwd_low_in, fwd_low),
                (inv_high_in, inv_high),
                (inv_low_in, inv_low),
                (short_in.at[pl.ds(pl.multiple_of(me * width, width), width)], short_taps),
                (short_in.at[far_columns], far_taps),
                (gate_in.at[:, far_columns], far_gate),
                (value_in.at[:, far_columns], far_value),
                (weight_in.at[pl.ds(me * heads, heads)], head_weight),
            )
        )
    ]
    for copy in tables:
        copy.start()
    my_rows = pl.ds(pl.multiple_of(me * rows, rows), rows)
    my_columns = pl.ds(pl.multiple_of(me * width, width), width)
    own = [
        pltpu.make_async_copy(stream.at[:, my_columns], held.at[a, my_rows], own_sem.at[a])
        for a, stream in enumerate(streams)
    ]
    for copy in own:
        copy.start()

    barrier = pltpu.get_barrier_semaphore()
    siblings = [lax.rem(my_group + step, groups) for step in range(1, groups)]
    for peer in peers:
        pl.semaphore_signal(
            barrier, inc=1, device_id={"seq": peer}, device_id_type=pl.DeviceIdType.MESH
        )
    for sibling in siblings:
        pl.semaphore_signal(
            barrier, inc=1, device_id={"groups": sibling}, device_id_type=pl.DeviceIdType.MESH
        )
    pl.semaphore_wait(barrier, len(peers) + len(siblings))

    def block_of(index):
        return pl.ds(pl.multiple_of(index * rows, rows), rows)

    def exchange(a, slot, peer, source, first, breadth):
        there = pl.ds(pl.multiple_of(peer * width + first, HEAD_DIM), breadth)
        here = pl.ds(pl.multiple_of(first, HEAD_DIM), breadth)
        return pltpu.make_async_remote_copy(
            src_ref=streams[a].at[:, there],
            dst_ref=held.at[a, block_of(source), here],
            send_sem=send_sem.at[slot, peer],
            recv_sem=recv_sem.at[slot, source],
            device_id={"seq": peer},
            device_id_type=pl.DeviceIdType.MESH,
        )

    def pass_on(step, source):
        here = pl.ds(pl.multiple_of(my_group * share, HEAD_DIM), share)
        return pltpu.make_async_remote_copy(
            src_ref=held.at[LONG, block_of(source), here],
            dst_ref=held.at[LONG, block_of(source), here],
            send_sem=pass_send.at[step, source],
            recv_sem=pass_recv.at[step, source],
            device_id={"groups": siblings[step]},
            device_id_type=pl.DeviceIdType.MESH,
        )

    def long_part(peer):
        return (0, width) if peer is partner else (my_group * share, share)

    halo = pltpu.make_async_remote_copy(
        src_ref=gate_in.at[:, far_columns],
        dst_ref=far_before,
        send_sem=halo_sem.at[0],
        recv_sem=halo_sem.at[1],
        device_id={"seq": partner},
        device_id_type=pl.DeviceIdType.MESH,
    )

    def send_mixed(peer, source):
        there = pl.ds(pl.multiple_of(lax.rem(peer, 2) * width, width), width)
        return pltpu.make_async_remote_copy(
            src_ref=far_mixed.at[:, there],
            dst_ref=mixed.at[block_of(source)],
            send_sem=send_sem.at[3, peer],
            recv_sem=recv_sem.at[3, source],
            device_id={"seq": peer},
            device_id_type=pl.DeviceIdType.MESH,
        )

    @pl.when(lax.rem(me, 2) == 0)
    def _():
        halo.start()

    sent = []
    for peer in peers:
        sent.append(exchange(LONG, 0, peer, me, *long_part(peer)))
    for a, slot in ((GATE, 1), (VALUE, 2)):
        sent.append(exchange(a, slot, partner, me, 0, width))
    for copy in sent:
        copy.start()
    raw_gate = [exchange(GATE, 1, peer, me, 0, width) for peer in far]
    raw_value = [exchange(VALUE, 2, peer, me, 0, width) for peer in far]
    sent_mixed = [send_mixed(peer, me) for peer in far]
    sends_gate = jnp.logical_or(me == 1, me == 2)
    sends_value = me == 2

    @pl.when(sends_gate)
    def _():
        for copy in raw_gate:
            copy.start()

    @pl.when(sends_value)
    def _():
        for copy in raw_value:
            copy.start()

    def arrive(a, slot, first=0, breadth=width):
        for peer in peers:
            exchange(a, slot, peer, peer, first, breadth).wait_recv()

    for copy in tables:
        copy.wait()

    def forward(signal):
        depth = signal.shape[0]
        both = dot(fwd_high[:, :depth], signal) + dot(fwd_low[:, :depth], signal)
        return both[:rows], both[rows:]

    def backward(re, im):
        re_high, re_low = split_pair(re)
        im_high, im_low = split_pair(im)
        high = jnp.concatenate([re_high, im_high], axis=0)
        low = jnp.concatenate([re_low, im_low], axis=0)
        return dot(inv_high[...], high) + (dot(inv_low[...], high) + dot(inv_high[...], low))

    def factor_parts(re, im):
        first = lax.broadcasted_iota(jnp.int32, re.shape, 0) == 0
        return re, jnp.where(first, 0.0, im), jnp.where(first, im, re)

    def window(a, block):
        now = held[a, block * rows : (block + 1) * rows]
        if block == 0:
            return now
        return jnp.concatenate([now, held[a, (block - 1) * rows : block * rows]], axis=0)

    last = ((1,), (1,))

    def taps_parts(taps):
        high, low = split_pair(taps[...])
        both = dot(fwd_high[:, :TAPS], high, last) + (
            dot(fwd_low[:, :TAPS], high, last) + dot(fwd_high[:, :TAPS], low, last)
        )
        return factor_parts(both[:rows], both[rows:])

    def smooth(signal, parts):
        re, im = forward(signal)
        re_part, im_part, nyq_part = parts
        return backward(re * re_part - im * im_part, re * im_part + im * nyq_part)

    @pl.when(me == 0)
    def _():
        far_before[...] = jnp.zeros_like(far_before)

    @pl.when(jnp.logical_not(sends_value))
    def _():
        far_parts = taps_parts(far_taps)

        @pl.when(lax.rem(me, 2) == 1)
        def _():
            halo.wait_recv()

        filtered = smooth(jnp.concatenate([far_gate[...], far_before[...]], axis=0), far_parts)
        far_mixed[...] = (filtered * far_value[...].astype(jnp.float32)).astype(jnp.bfloat16)
        for copy in sent_mixed:
            copy.start()

    late_sent = []
    for head in range(heads):
        for a, slot in ((KEY, 4 + 2 * head), (VAL, 5 + 2 * head)):
            for peer in peers:
                late_sent.append(exchange(a, slot, peer, me, head * HEAD_DIM, HEAD_DIM))
    for copy in late_sent:
        copy.start()

    passed = []
    for peer in peers:
        exchange(LONG, 0, peer, peer, *long_part(peer)).wait_recv()
        if peer is not partner:
            for step in range(groups - 1):
                passed.append(pass_on(step, peer))
                passed[-1].start()

    parts = taps_parts(short_taps)
    own[GATE].wait()
    for source in (partner, 2 - late):
        exchange(GATE, 1, source, source, 0, width).wait_recv()

    def smooth_blocks(*blocks):
        for block in blocks:
            smoothed[block] = smooth(window(GATE, block), parts)

    def mix_blocks(*blocks):
        for block in blocks:
            here = slice(block * rows, (block + 1) * rows)
            mixed[here] = (smoothed[block] * held[VALUE, here].astype(jnp.float32)).astype(
                jnp.bfloat16
            )

    smooth_blocks(2)

    @pl.when(late == 0)
    def _():
        smooth_blocks(0, 1)

    @pl.when(late == 1)
    def _():
        smooth_blocks(3)

    own[LONG].wait()
    for copy in passed:
        copy.wait_recv()
    for block in range(count):
        re, im, nyq = factor_parts(*forward(window(LONG, block)))
        grid_re[block], grid_im[block], grid_nyq[block] = re, im, nyq

    own[VALUE].wait()
    exchange(VALUE, 2, partner, partner, 0, width).wait_recv()

    @pl.when(late == 0)
    def _():
        exchange(VALUE, 2, 2, 2, 0, width).wait_recv()
        mix_blocks(0, 1, 2)
        send_mixed(3, 3).wait_recv()

    @pl.when(late == 1)
    def _():
        mix_blocks(2, 3)
        send_mixed(0, 0).wait_recv()
        send_mixed(1, 1).wait_recv()

    for block in range(count):
        sig_re[block], sig_im[block] = forward(mixed[block * rows : (block + 1) * rows])

    for block in range(count):
        re = im = None
        for source in range(block + 1):
            lag = block - source
            s_re, s_im = sig_re[source], sig_im[source]
            re_term = s_re * grid_re[lag] - s_im * grid_im[lag]
            im_term = s_re * grid_im[lag] + s_im * grid_nyq[lag]
            re = re_term if re is None else re + re_term
            im = im_term if im is None else im + im_term
        conv[block * rows : (block + 1) * rows] = backward(re, im).astype(jnp.bfloat16)

    def give_back(block, head, peer):
        columns = pl.ds(pl.multiple_of(me * width + head * HEAD_DIM, HEAD_DIM), HEAD_DIM)
        return pltpu.make_async_remote_copy(
            src_ref=result.at[head, block * rows : (block + 1) * rows],
            dst_ref=out.at[:, columns],
            send_sem=out_send.at[block, head],
            recv_sem=out_recv.at[me, head],
            device_id={"seq": peer},
            device_id_type=pl.DeviceIdType.MESH,
        )

    def keep(block, head):
        columns = pl.ds(pl.multiple_of(me * width + head * HEAD_DIM, HEAD_DIM), HEAD_DIM)
        return pltpu.make_async_copy(
            result.at[head, block * rows : (block + 1) * rows], out.at[:, columns], out_own.at[head]
        )

    scale = 1.0 / math.sqrt(HEAD_DIM)
    own[KEY].wait()
    own[VAL].wait()
    for head in range(heads):
        arrive(KEY, 4 + 2 * head, head * HEAD_DIM, HEAD_DIM)
        columns = slice(head * HEAD_DIM, (head + 1) * HEAD_DIM)
        for block in range(count):
            here = slice(block * rows, (block + 1) * rows)
            past = (block + 1) * rows
            query = dot(conv[here, columns], head_weight[head]).astype(jnp.bfloat16)
            scores = dot(query, held[KEY, :past, columns], last) * scale
            key_pos = lax.broadcasted_iota(jnp.int32, scores.shape, 1)
            query_pos = block * rows + lax.broadcasted_iota(jnp.int32, scores.shape, 0)
            allowed = key_pos <= query_pos
            scores = jnp.where(allowed, scores, -1e30)
            peak = jnp.max(scores, axis=1, keepdims=True)
            share = jnp.where(allowed, jnp.exp(scores - peak), 0.0)
            sums[head, here] = jnp.broadcast_to(
                jnp.sum(share, axis=1, keepdims=True), (rows, HEAD_DIM)
            )
            weights[head, here, :past] = share.astype(jnp.bfloat16)

        arrive(VAL, 5 + 2 * head, head * HEAD_DIM, HEAD_DIM)
        for block in reversed(range(count)):
            here = slice(block * rows, (block + 1) * rows)
            past = (block + 1) * rows
            columns = slice(head * HEAD_DIM, (head + 1) * HEAD_DIM)
            product = dot(weights[head, here, :past], held[VAL, :past, columns])
            result[head, here] = (product / sums[head, here]).astype(jnp.bfloat16)

            @pl.when(me != block)
            def _():
                give_back(block, head, block).start()

            @pl.when(me == block)
            def _():
                keep(block, head).start()

    for copy in [*sent, *passed, *late_sent]:
        copy.wait_send()

    @pl.when(lax.rem(me, 2) == 0)
    def _():
        halo.wait_send()

    @pl.when(sends_gate)
    def _():
        for copy in raw_gate:
            copy.wait_send()

    @pl.when(sends_value)
    def _():
        for copy in raw_value:
            copy.wait_send()

    @pl.when(jnp.logical_not(sends_value))
    def _():
        for copy in sent_mixed:
            copy.wait_send()

    for head in range(heads):
        for peer in peers:
            columns = pl.ds(pl.multiple_of(peer * width + head * HEAD_DIM, HEAD_DIM), HEAD_DIM)
            pltpu.make_async_remote_copy(
                src_ref=result.at[head, :rows],
                dst_ref=out.at[:, columns],
                send_sem=out_send.at[0, head],
                recv_sem=out_recv.at[peer, head],
                device_id={"seq": peer},
                device_id_type=pl.DeviceIdType.MESH,
            ).wait_recv()
        for block in range(count):

            @pl.when(me != block)
            def _():
                give_back(block, head, block).wait_send()

            @pl.when(me == block)
            def _():
                keep(block, head).wait()


def head_shards(
    count,
    groups,
    gate_input,
    value_input,
    short_filter,
    long_filter,
    query_weight,
    key_matrix,
    value_matrix,
):
    rows, local_width = gate_input.shape
    width = local_width // count
    heads = width // HEAD_DIM
    length = count * rows
    forward, inverse_table = transform_tables(rows)
    forward = host_split(forward)
    inverse_table = host_split(inverse_table)
    bf16, f32 = jnp.bfloat16, jnp.float32
    return pl.pallas_call(
        functools.partial(block_kernel, count),
        out_shape=pltpu.VMEM((rows, local_width), bf16),
        in_specs=[pl.BlockSpec(memory_space=pl.ANY)] * 11,
        out_specs=pl.BlockSpec(memory_space=pltpu.VMEM),
        scratch_shapes=[
            pltpu.VMEM((5, length, width), bf16),
            pltpu.VMEM((width, TAPS), f32),
            pltpu.VMEM((heads, HEAD_DIM, HEAD_DIM), bf16),
            pltpu.VMEM((2 * rows, 2 * rows), bf16),
            pltpu.VMEM((2 * rows, 2 * rows), bf16),
            pltpu.VMEM((rows, 2 * rows), bf16),
            pltpu.VMEM((rows, 2 * rows), bf16),
            pltpu.VMEM((count, rows, width), f32),
            pltpu.VMEM((count, rows, width), f32),
            pltpu.VMEM((count, rows, width), f32),
            pltpu.VMEM((count, rows, width), f32),
            pltpu.VMEM((count, rows, width), f32),
            pltpu.VMEM((length, width), bf16),
            pltpu.VMEM((heads, length, length), bf16),
            pltpu.VMEM((heads, length, HEAD_DIM), f32),
            pltpu.VMEM((heads, length, HEAD_DIM), bf16),
            pltpu.VMEM((count, rows, width), f32),
            pltpu.VMEM((length, width), bf16),
            pltpu.VMEM((2 * width, TAPS), f32),
            pltpu.VMEM((rows, 2 * width), bf16),
            pltpu.VMEM((rows, 2 * width), bf16),
            pltpu.VMEM((rows, 2 * width), bf16),
            pltpu.VMEM((rows, 2 * width), bf16),
            pltpu.SemaphoreType.DMA((2,)),
            pltpu.SemaphoreType.DMA((groups - 1, count)),
            pltpu.SemaphoreType.DMA((groups - 1, count)),
            pltpu.SemaphoreType.DMA((4 + 2 * heads, count)),
            pltpu.SemaphoreType.DMA((4 + 2 * heads, count)),
            pltpu.SemaphoreType.DMA((5,)),
            pltpu.SemaphoreType.DMA((count, heads)),
            pltpu.SemaphoreType.DMA((count, heads)),
            pltpu.SemaphoreType.DMA((heads,)),
            pltpu.SemaphoreType.DMA((9,)),
        ],
        compiler_params=pltpu.CompilerParams(collective_id=0, has_side_effects=True),
    )(
        gate_input,
        value_input,
        long_filter,
        key_matrix,
        value_matrix,
        short_filter,
        query_weight,
        *forward,
        *inverse_table,
    )


def shards(count, groups, gate_input, *others):
    rows, local_width = gate_input.shape
    by_heads = local_width % (count * groups * HEAD_DIM) == 0
    by_rows = rows >= TAPS and rows % HEAD_DIM == 0
    two_pairs = count == 4
    if two_pairs and groups > 1 and by_heads and by_rows:
        return head_shards(count, groups, gate_input, *others)
    return general_shards(gate_input, *others)


def solution(mesh):
    in_specs = (
        P(("groups", "seq"), "chan"),
        P(("groups", "seq"), "chan"),
        P("chan", None),
        P("seq", "chan"),
        P("chan", None, None),
        P(("groups", "seq"), "chan"),
        P(("groups", "seq"), "chan"),
    )
    out_specs = P(("groups", "seq"), "chan")
    return jax.shard_map(
        functools.partial(shards, mesh.shape["seq"], mesh.shape["groups"]), mesh=mesh, in_specs=in_specs, out_specs=out_specs, check_vma=False)
```

```python
import functools
import math

import jax
import jax.numpy as jnp
import numpy as np
from jax import lax
from jax.experimental import pallas as pl
from jax.experimental.pallas import tpu as pltpu
from jax.sharding import PartitionSpec as P

HEAD_DIM = 128
TAPS = 128
RADIX = 128


HIGHEST = lax.Precision.HIGHEST


def shifted(value, axis, steps):
    count = lax.axis_size(axis)
    initial, last = (max(0, -steps), min(count, count - steps))
    return lax.ppermute(value, axis, [(source, source + steps) for source in range(initial, last)])


def unit_table(height, breadth, modulus, orient):
    product = (
        lax.broadcasted_iota(jnp.int32, (height, breadth), 0)
        * lax.broadcasted_iota(jnp.int32, (height, breadth), 1)
        % modulus
    )
    angles = 2.0 * math.pi / modulus * product.astype(jnp.float32)
    return (jnp.cos(angles), orient * jnp.sin(angles))


def block_table(factor, orient):
    inner_re, inner_im = unit_table(factor, factor, factor, orient)
    upper = jnp.concatenate([inner_re, inner_im], axis=1)
    lower = jnp.concatenate([-inner_im, inner_re], axis=1)
    return jnp.concatenate([upper, lower], axis=0)


def spectrum(signal, factor):
    channels, length = signal.shape
    full_length = 2 * length
    column_count = full_length // factor
    folded = signal.reshape(channels, column_count // 2, factor)
    outer_re, outer_im = unit_table(column_count, column_count // 2, column_count, -1.0)
    outer_both = jnp.concatenate([outer_re, outer_im], axis=0)
    first = jnp.einsum("kn,cnm->ckm", outer_both, folded, precision=HIGHEST)
    first_re = first[:, :column_count]
    first_im = first[:, column_count:]
    twist_re, twist_im = unit_table(column_count, factor, full_length, -1.0)
    mid_re = first_re * twist_re - first_im * twist_im
    mid_im = first_re * twist_im + first_im * twist_re
    joined = jnp.concatenate([mid_re, mid_im], axis=2)
    return jnp.einsum("ckn,nm->ckm", joined, block_table(factor, -1.0), precision=HIGHEST)


def inverse(spec_both, factor, length):
    channels = spec_both.shape[0]
    full_length = 2 * length
    column_count = full_length // factor
    mid = jnp.einsum("ckm,mn->ckn", spec_both, block_table(factor, 1.0), precision=HIGHEST)
    mid_re = mid[:, :, :factor]
    mid_im = mid[:, :, factor:]
    twist_re, twist_im = unit_table(column_count, factor, full_length, 1.0)
    turn_re = mid_re * twist_re - mid_im * twist_im
    turn_im = mid_re * twist_im + mid_im * twist_re
    outer_re, outer_im = unit_table(column_count // 2, column_count, column_count, 1.0)
    outer_both = jnp.concatenate([outer_re, -outer_im], axis=1)
    turned = jnp.concatenate([turn_re, turn_im], axis=1)
    result = jnp.einsum("nk,ckm->cnm", outer_both, turned, precision=HIGHEST)
    return result.reshape(channels, length) / full_length


def general_shards(
    gate_input, value_input, short_filter, long_filter, query_weight, key_matrix, value_matrix
):
    seq_rows, local_width = gate_input.shape
    last_rows = gate_input[seq_rows - (TAPS - 1) :]
    earlier = shifted(last_rows, "seq", 1)
    padded = jnp.concatenate([earlier, gate_input], axis=0).astype(jnp.float32)
    kernel = short_filter[:, ::-1].T[:, None, :]
    smoothed = lax.conv_general_dilated(
        padded[None],
        kernel,
        (1,),
        "VALID",
        dimension_numbers=("NHC", "HIO", "NHC"),
        feature_group_count=local_width,
        precision=HIGHEST,
    )[0]
    mixed_input = (smoothed * value_input.astype(jnp.float32)).astype(jnp.bfloat16)
    signal, kernel_line = (
        lax.all_to_all(mixed_input.T, "seq", split_axis=0, concat_axis=1, tiled=True),
        lax.all_to_all(long_filter.T, "seq", split_axis=0, concat_axis=1, tiled=True),
    )
    length = signal.shape[1]
    signal_both = spectrum(signal.astype(jnp.float32), RADIX)
    kernel_both = spectrum(kernel_line.astype(jnp.float32), RADIX)
    signal_re = signal_both[:, :, :RADIX]
    signal_im = signal_both[:, :, RADIX:]
    kernel_re = kernel_both[:, :, :RADIX]
    kernel_im = kernel_both[:, :, RADIX:]
    joint = jnp.concatenate(
        [
            signal_re * kernel_re - signal_im * kernel_im,
            signal_re * kernel_im + signal_im * kernel_re,
        ],
        axis=2,
    )
    conv_line = inverse(joint, RADIX, length).astype(jnp.bfloat16)
    my_index = lax.axis_index("seq")
    group_firsts = [my_index * seq_rows]
    conv_columns = lax.all_to_all(conv_line, "seq", split_axis=1, concat_axis=0, tiled=True)
    heads_here = local_width // HEAD_DIM
    conv_heads = conv_columns.reshape(heads_here, HEAD_DIM, seq_rows)
    query_heads = jnp.einsum(
        "hds,hde->hse", conv_heads, query_weight, preferred_element_type=jnp.float32
    ).astype(jnp.bfloat16)
    group_count = len(group_firsts)
    query_groups = [query_heads]
    key_heads = key_matrix.reshape(seq_rows, heads_here, HEAD_DIM).transpose(1, 0, 2)
    value_heads = value_matrix.reshape(seq_rows, heads_here, HEAD_DIM).transpose(1, 0, 2)
    score_scale = 1.0 / math.sqrt(HEAD_DIM)

    def attend_group(running, group_query, group_first, key_block, value_block, first_row):
        block_rows = key_block.shape[1]

        def compute(current):
            peak_value, weight_sum, weighted = current
            scores = (
                jnp.einsum(
                    "hqd,hkd->hqk", group_query, key_block, preferred_element_type=jnp.float32
                )
                * score_scale
            )
            key_pos = first_row + lax.iota(jnp.int32, block_rows)
            query_pos = group_first + lax.iota(jnp.int32, seq_rows)
            allowed = (key_pos[None, :] <= query_pos[:, None])[None]
            scores = jnp.where(allowed, scores, -1e30)
            new_peak = jnp.maximum(peak_value, jnp.max(scores, axis=2))
            weights = jnp.where(allowed, jnp.exp(scores - new_peak[:, :, None]), 0.0)
            rescale = jnp.exp(peak_value - new_peak)
            weight_sum = weight_sum * rescale + jnp.sum(weights, axis=2)
            weighted = weighted * rescale[:, :, None] + jnp.einsum(
                "hqk,hkd->hqd",
                weights.astype(jnp.bfloat16),
                value_block,
                preferred_element_type=jnp.float32,
            )
            return (new_peak, weight_sum, weighted)

        live = first_row <= group_first + seq_rows - 1
        return lax.cond(live, compute, lambda current: current, running)

    def attend(states, key_block, value_block, first_row):
        return tuple(
            (
                attend_group(
                    states[g], query_groups[g], group_firsts[g], key_block, value_block, first_row
                )
                for g in range(group_count)
            )
        )

    one_state = (
        jnp.full((heads_here, seq_rows), -1e30, jnp.float32),
        jnp.zeros((heads_here, seq_rows), jnp.float32),
        jnp.zeros((heads_here, seq_rows, HEAD_DIM), jnp.float32),
    )
    initial = tuple((one_state for g in range(group_count)))
    running = initial
    key_piece = lax.all_gather(key_heads, "seq", axis=1, tiled=True)
    value_piece = lax.all_gather(value_heads, "seq", axis=1, tiled=True)
    piece_rows = key_piece.shape[1]
    block_rows = 512
    block_count = piece_rows // block_rows
    key_blocks = key_piece.reshape(heads_here, block_count, block_rows, HEAD_DIM).transpose(
        1, 0, 2, 3
    )
    value_blocks = value_piece.reshape(heads_here, block_count, block_rows, HEAD_DIM).transpose(
        1, 0, 2, 3
    )

    def advance(current, element):
        key_block, value_block, position = element
        return (attend(current, key_block, value_block, position * block_rows), None)

    running, _ = lax.scan(
        advance, running, (key_blocks, value_blocks, lax.iota(jnp.int32, block_count))
    )
    outputs = [state[2] / state[1][:, :, None] for state in running]
    result = outputs[0]
    attended_rows = result.transpose(1, 0, 2).reshape(seq_rows, local_width).astype(jnp.bfloat16)
    return attended_rows


def split_pair(array):
    high = array.astype(jnp.bfloat16)
    return high, (array - high.astype(jnp.float32)).astype(jnp.bfloat16)


def transform_tables(rows):
    full = 2 * rows
    turn = np.arange(rows)[:, None] * np.arange(full)[None, :] % full
    angle = 2.0 * np.pi / full * turn
    forward = np.concatenate([np.cos(angle), -np.sin(angle)], axis=0)
    forward[rows] = 1.0 - 2.0 * (np.arange(full) % 2)
    weight = np.full((full,), 2.0 / full)
    weight[0] = weight[rows] = 1.0 / full
    backward = (forward[:, :rows] * weight[:, None]).T
    return forward, backward


def host_split(table):
    high = table.astype(jnp.bfloat16)
    low = (table - high.astype(np.float64)).astype(jnp.bfloat16)
    return jnp.asarray(high), jnp.asarray(low)


def dot(a, b, contract=((1,), (0,))):
    return lax.dot_general(a, b, (contract, ((), ())), preferred_element_type=jnp.float32)


def block_kernel(
    count,
    gate_in,
    value_in,
    long_in,
    key_in,
    val_in,
    short_in,
    weight_in,
    fwd_high_in,
    fwd_low_in,
    inv_high_in,
    inv_low_in,
    out,
    held,
    short_taps,
    head_weight,
    fwd_high,
    fwd_low,
    inv_high,
    inv_low,
    grid_re,
    grid_im,
    grid_nyq,
    sig_re,
    sig_im,
    conv,
    weights,
    sums,
    result,
    smoothed,
    mixed,
    far_taps,
    far_gate,
    far_before,
    far_value,
    far_mixed,
    halo_sem,
    pass_send,
    pass_recv,
    send_sem,
    recv_sem,
    own_sem,
    out_send,
    out_recv,
    out_own,
    table_sem,
):
    me = lax.axis_index("seq")
    rows = gate_in.shape[0]
    width = held.shape[2]
    heads = width // HEAD_DIM
    streams = (gate_in, value_in, long_in, key_in, val_in)
    GATE, VALUE, LONG, KEY, VAL = range(5)
    groups = lax.axis_size("groups")
    my_group = lax.axis_index("groups")
    share = width // groups

    def flip(index):
        return index + 1 - 2 * lax.rem(index, 2)

    partner = flip(me)
    opposite = lax.rem(me + 2, count)
    far = [opposite, flip(opposite)]
    peers = [*far, partner]
    late = me // 2
    far_columns = pl.ds(pl.multiple_of((1 - late) * 2 * width, 2 * width), 2 * width)

    tables = [
        pltpu.make_async_copy(source, target, table_sem.at[i])
        for i, (source, target) in enumerate(
            (
                (fwd_high_in, fwd_high),
                (fwd_low_in, fwd_low),
                (inv_high_in, inv_high),
                (inv_low_in, inv_low),
                (short_in.at[pl.ds(pl.multiple_of(me * width, width), width)], short_taps),
                (short_in.at[far_columns], far_taps),
                (gate_in.at[:, far_columns], far_gate),
                (value_in.at[:, far_columns], far_value),
                (weight_in.at[pl.ds(me * heads, heads)], head_weight),
            )
        )
    ]
    for copy in tables:
        copy.start()
    my_rows = pl.ds(pl.multiple_of(me * rows, rows), rows)
    my_columns = pl.ds(pl.multiple_of(me * width, width), width)
    own = [
        pltpu.make_async_copy(stream.at[:, my_columns], held.at[a, my_rows], own_sem.at[a])
        for a, stream in enumerate(streams)
    ]
    for copy in own:
        copy.start()

    barrier = pltpu.get_barrier_semaphore()
    siblings = [lax.rem(my_group + step, groups) for step in range(1, groups)]
    for peer in peers:
        pl.semaphore_signal(
            barrier, inc=1, device_id={"seq": peer}, device_id_type=pl.DeviceIdType.MESH
        )
    for sibling in siblings:
        pl.semaphore_signal(
            barrier, inc=1, device_id={"groups": sibling}, device_id_type=pl.DeviceIdType.MESH
        )
    pl.semaphore_wait(barrier, len(peers) + len(siblings))

    def block_of(index):
        return pl.ds(pl.multiple_of(index * rows, rows), rows)

    def exchange(a, slot, peer, source, first, breadth):
        there = pl.ds(pl.multiple_of(peer * width + first, HEAD_DIM), breadth)
        here = pl.ds(pl.multiple_of(first, HEAD_DIM), breadth)
        return pltpu.make_async_remote_copy(
            src_ref=streams[a].at[:, there],
            dst_ref=held.at[a, block_of(source), here],
            send_sem=send_sem.at[slot, peer],
            recv_sem=recv_sem.at[slot, source],
            device_id={"seq": peer},
            device_id_type=pl.DeviceIdType.MESH,
        )

    def pass_on(step, source):
        here = pl.ds(pl.multiple_of(my_group * share, HEAD_DIM), share)
        return pltpu.make_async_remote_copy(
            src_ref=held.at[LONG, block_of(source), here],
            dst_ref=held.at[LONG, block_of(source), here],
            send_sem=pass_send.at[step, source],
            recv_sem=pass_recv.at[step, source],
            device_id={"groups": siblings[step]},
            device_id_type=pl.DeviceIdType.MESH,
        )

    def long_part(peer):
        return (0, width) if peer is partner else (my_group * share, share)

    halo = pltpu.make_async_remote_copy(
        src_ref=gate_in.at[:, far_columns],
        dst_ref=far_before,
        send_sem=halo_sem.at[0],
        recv_sem=halo_sem.at[1],
        device_id={"seq": partner},
        device_id_type=pl.DeviceIdType.MESH,
    )

    def send_mixed(peer, source):
        there = pl.ds(pl.multiple_of(lax.rem(peer, 2) * width, width), width)
        return pltpu.make_async_remote_copy(
            src_ref=far_mixed.at[:, there],
            dst_ref=mixed.at[block_of(source)],
            send_sem=send_sem.at[3, peer],
            recv_sem=recv_sem.at[3, source],
            device_id={"seq": peer},
            device_id_type=pl.DeviceIdType.MESH,
        )

    @pl.when(lax.rem(me, 2) == 0)
    def _():
        halo.start()

    sent = []
    for peer in peers:
        sent.append(exchange(LONG, 0, peer, me, *long_part(peer)))
    for a, slot in ((GATE, 1), (VALUE, 2)):
        sent.append(exchange(a, slot, partner, me, 0, width))
    for copy in sent:
        copy.start()
    raw_gate = [exchange(GATE, 1, peer, me, 0, width) for peer in far]
    raw_value = [exchange(VALUE, 2, peer, me, 0, width) for peer in far]
    sent_mixed = [send_mixed(peer, me) for peer in far]
    sends_gate = jnp.logical_or(me == 1, me == 2)
    sends_value = me == 2

    @pl.when(sends_gate)
    def _():
        for copy in raw_gate:
            copy.start()

    @pl.when(sends_value)
    def _():
        for copy in raw_value:
            copy.start()

    def arrive(a, slot, first=0, breadth=width):
        for peer in peers:
            exchange(a, slot, peer, peer, first, breadth).wait_recv()

    for copy in tables:
        copy.wait()

    def forward(signal):
        depth = signal.shape[0]
        both = dot(fwd_high[:, :depth], signal) + dot(fwd_low[:, :depth], signal)
        return both[:rows], both[rows:]

    def backward(re, im):
        re_high, re_low = split_pair(re)
        im_high, im_low = split_pair(im)
        high = jnp.concatenate([re_high, im_high], axis=0)
        low = jnp.concatenate([re_low, im_low], axis=0)
        return dot(inv_high[...], high) + (dot(inv_low[...], high) + dot(inv_high[...], low))

    def factor_parts(re, im):
        first = lax.broadcasted_iota(jnp.int32, re.shape, 0) == 0
        return re, jnp.where(first, 0.0, im), jnp.where(first, im, re)

    def window(a, block):
        now = held[a, block * rows : (block + 1) * rows]
        if block == 0:
            return now
        return jnp.concatenate([now, held[a, (block - 1) * rows : block * rows]], axis=0)

    last = ((1,), (1,))

    def taps_parts(taps):
        high, low = split_pair(taps[...])
        both = dot(fwd_high[:, :TAPS], high, last) + (
            dot(fwd_low[:, :TAPS], high, last) + dot(fwd_high[:, :TAPS], low, last)
        )
        return factor_parts(both[:rows], both[rows:])

    def smooth(signal, parts):
        re, im = forward(signal)
        re_part, im_part, nyq_part = parts
        return backward(re * re_part - im * im_part, re * im_part + im * nyq_part)

    @pl.when(me == 0)
    def _():
        far_before[...] = jnp.zeros_like(far_before)

    @pl.when(jnp.logical_not(sends_value))
    def _():
        far_parts = taps_parts(far_taps)

        @pl.when(lax.rem(me, 2) == 1)
        def _():
            halo.wait_recv()

        filtered = smooth(jnp.concatenate([far_gate[...], far_before[...]], axis=0), far_parts)
        far_mixed[...] = (filtered * far_value[...].astype(jnp.float32)).astype(jnp.bfloat16)
        for copy in sent_mixed:
            copy.start()

    late_sent = []
    for head in range(heads):
        for a, slot in ((KEY, 4 + 2 * head), (VAL, 5 + 2 * head)):
            for peer in peers:
                late_sent.append(exchange(a, slot, peer, me, head * HEAD_DIM, HEAD_DIM))
    for copy in late_sent:
        copy.start()

    passed = []
    for peer in peers:
        exchange(LONG, 0, peer, peer, *long_part(peer)).wait_recv()
        if peer is not partner:
            for step in range(groups - 1):
                passed.append(pass_on(step, peer))
                passed[-1].start()

    parts = taps_parts(short_taps)
    own[GATE].wait()
    for source in (partner, 2 - late):
        exchange(GATE, 1, source, source, 0, width).wait_recv()

    def smooth_blocks(*blocks):
        for block in blocks:
            smoothed[block] = smooth(window(GATE, block), parts)

    def mix_blocks(*blocks):
        for block in blocks:
            here = slice(block * rows, (block + 1) * rows)
            mixed[here] = (smoothed[block] * held[VALUE, here].astype(jnp.float32)).astype(
                jnp.bfloat16
            )

    smooth_blocks(2)

    @pl.when(late == 0)
    def _():
        smooth_blocks(0, 1)

    @pl.when(late == 1)
    def _():
        smooth_blocks(3)

    own[LONG].wait()
    for copy in passed:
        copy.wait_recv()
    for block in range(count):
        re, im, nyq = factor_parts(*forward(window(LONG, block)))
        grid_re[block], grid_im[block], grid_nyq[block] = re, im, nyq

    own[VALUE].wait()
    exchange(VALUE, 2, partner, partner, 0, width).wait_recv()

    @pl.when(late == 0)
    def _():
        exchange(VALUE, 2, 2, 2, 0, width).wait_recv()
        mix_blocks(0, 1, 2)
        send_mixed(3, 3).wait_recv()

    @pl.when(late == 1)
    def _():
        mix_blocks(2, 3)
        send_mixed(0, 0).wait_recv()
        send_mixed(1, 1).wait_recv()

    for block in range(count):
        sig_re[block], sig_im[block] = forward(mixed[block * rows : (block + 1) * rows])

    for block in range(count):
        re = im = None
        for source in range(block + 1):
            lag = block - source
            s_re, s_im = sig_re[source], sig_im[source]
            re_term = s_re * grid_re[lag] - s_im * grid_im[lag]
            im_term = s_re * grid_im[lag] + s_im * grid_nyq[lag]
            re = re_term if re is None else re + re_term
            im = im_term if im is None else im + im_term
        conv[block * rows : (block + 1) * rows] = backward(re, im).astype(jnp.bfloat16)

    def give_back(block, head, peer):
        columns = pl.ds(pl.multiple_of(me * width + head * HEAD_DIM, HEAD_DIM), HEAD_DIM)
        return pltpu.make_async_remote_copy(
            src_ref=result.at[head, block * rows : (block + 1) * rows],
            dst_ref=out.at[:, columns],
            send_sem=out_send.at[block, head],
            recv_sem=out_recv.at[me, head],
            device_id={"seq": peer},
            device_id_type=pl.DeviceIdType.MESH,
        )

    def keep(block, head):
        columns = pl.ds(pl.multiple_of(me * width + head * HEAD_DIM, HEAD_DIM), HEAD_DIM)
        return pltpu.make_async_copy(
            result.at[head, block * rows : (block + 1) * rows], out.at[:, columns], out_own.at[head]
        )

    scale = 1.0 / math.sqrt(HEAD_DIM)
    own[KEY].wait()
    own[VAL].wait()
    for head in range(heads):
        arrive(KEY, 4 + 2 * head, head * HEAD_DIM, HEAD_DIM)
        columns = slice(head * HEAD_DIM, (head + 1) * HEAD_DIM)
        for block in range(count):
            here = slice(block * rows, (block + 1) * rows)
            past = (block + 1) * rows
            query = dot(conv[here, columns], head_weight[head]).astype(jnp.bfloat16)
            scores = dot(query, held[KEY, :past, columns], last) * scale
            key_pos = lax.broadcasted_iota(jnp.int32, scores.shape, 1)
            query_pos = block * rows + lax.broadcasted_iota(jnp.int32, scores.shape, 0)
            allowed = key_pos <= query_pos
            scores = jnp.where(allowed, scores, -1e30)
            peak = jnp.max(scores, axis=1, keepdims=True)
            share = jnp.where(allowed, jnp.exp(scores - peak), 0.0)
            sums[head, here] = jnp.broadcast_to(
                jnp.sum(share, axis=1, keepdims=True), (rows, HEAD_DIM)
            )
            weights[head, here, :past] = share.astype(jnp.bfloat16)

        def finish(block):
            here = slice(block * rows, (block + 1) * rows)
            past = (block + 1) * rows
            columns = slice(head * HEAD_DIM, (head + 1) * HEAD_DIM)
            product = dot(weights[head, here, :past], held[VAL, :past, columns])
            result[head, here] = (product / sums[head, here]).astype(jnp.bfloat16)

            @pl.when(me != block)
            def _():
                give_back(block, head, block).start()

            @pl.when(me == block)
            def _():
                keep(block, head).start()

        def value_from(source):
            exchange(
                VAL, 5 + 2 * head, source, source, head * HEAD_DIM, HEAD_DIM
            ).wait_recv()

        value_from(partner)

        @pl.when(late == 0)
        def _():
            for block in (2, 3):
                value_from(block)
                finish(block)
            finish(1)
            finish(0)

        @pl.when(late == 1)
        def _():
            for block in (0, 1):
                value_from(block)
                finish(block)
            finish(2)
            finish(3)

    for copy in [*sent, *passed, *late_sent]:
        copy.wait_send()

    @pl.when(lax.rem(me, 2) == 0)
    def _():
        halo.wait_send()

    @pl.when(sends_gate)
    def _():
        for copy in raw_gate:
            copy.wait_send()

    @pl.when(sends_value)
    def _():
        for copy in raw_value:
            copy.wait_send()

    @pl.when(jnp.logical_not(sends_value))
    def _():
        for copy in sent_mixed:
            copy.wait_send()

    for head in range(heads):
        for peer in peers:
            columns = pl.ds(pl.multiple_of(peer * width + head * HEAD_DIM, HEAD_DIM), HEAD_DIM)
            pltpu.make_async_remote_copy(
                src_ref=result.at[head, :rows],
                dst_ref=out.at[:, columns],
                send_sem=out_send.at[0, head],
                recv_sem=out_recv.at[peer, head],
                device_id={"seq": peer},
                device_id_type=pl.DeviceIdType.MESH,
            ).wait_recv()
        for block in range(count):

            @pl.when(me != block)
            def _():
                give_back(block, head, block).wait_send()

            @pl.when(me == block)
            def _():
                keep(block, head).wait()


def head_shards(
    count,
    groups,
    gate_input,
    value_input,
    short_filter,
    long_filter,
    query_weight,
    key_matrix,
    value_matrix,
):
    rows, local_width = gate_input.shape
    width = local_width // count
    heads = width // HEAD_DIM
    length = count * rows
    forward, inverse_table = transform_tables(rows)
    forward = host_split(forward)
    inverse_table = host_split(inverse_table)
    bf16, f32 = jnp.bfloat16, jnp.float32
    return pl.pallas_call(
        functools.partial(block_kernel, count),
        out_shape=pltpu.VMEM((rows, local_width), bf16),
        in_specs=[pl.BlockSpec(memory_space=pl.ANY)] * 11,
        out_specs=pl.BlockSpec(memory_space=pltpu.VMEM),
        scratch_shapes=[
            pltpu.VMEM((5, length, width), bf16),
            pltpu.VMEM((width, TAPS), f32),
            pltpu.VMEM((heads, HEAD_DIM, HEAD_DIM), bf16),
            pltpu.VMEM((2 * rows, 2 * rows), bf16),
            pltpu.VMEM((2 * rows, 2 * rows), bf16),
            pltpu.VMEM((rows, 2 * rows), bf16),
            pltpu.VMEM((rows, 2 * rows), bf16),
            pltpu.VMEM((count, rows, width), f32),
            pltpu.VMEM((count, rows, width), f32),
            pltpu.VMEM((count, rows, width), f32),
            pltpu.VMEM((count, rows, width), f32),
            pltpu.VMEM((count, rows, width), f32),
            pltpu.VMEM((length, width), bf16),
            pltpu.VMEM((heads, length, length), bf16),
            pltpu.VMEM((heads, length, HEAD_DIM), f32),
            pltpu.VMEM((heads, length, HEAD_DIM), bf16),
            pltpu.VMEM((count, rows, width), f32),
            pltpu.VMEM((length, width), bf16),
            pltpu.VMEM((2 * width, TAPS), f32),
            pltpu.VMEM((rows, 2 * width), bf16),
            pltpu.VMEM((rows, 2 * width), bf16),
            pltpu.VMEM((rows, 2 * width), bf16),
            pltpu.VMEM((rows, 2 * width), bf16),
            pltpu.SemaphoreType.DMA((2,)),
            pltpu.SemaphoreType.DMA((groups - 1, count)),
            pltpu.SemaphoreType.DMA((groups - 1, count)),
            pltpu.SemaphoreType.DMA((4 + 2 * heads, count)),
            pltpu.SemaphoreType.DMA((4 + 2 * heads, count)),
            pltpu.SemaphoreType.DMA((5,)),
            pltpu.SemaphoreType.DMA((count, heads)),
            pltpu.SemaphoreType.DMA((count, heads)),
            pltpu.SemaphoreType.DMA((heads,)),
            pltpu.SemaphoreType.DMA((9,)),
        ],
        compiler_params=pltpu.CompilerParams(collective_id=0, has_side_effects=True),
    )(
        gate_input,
        value_input,
        long_filter,
        key_matrix,
        value_matrix,
        short_filter,
        query_weight,
        *forward,
        *inverse_table,
    )


def shards(count, groups, gate_input, *others):
    rows, local_width = gate_input.shape
    by_heads = local_width % (count * groups * HEAD_DIM) == 0
    by_rows = rows >= TAPS and rows % HEAD_DIM == 0
    two_pairs = count == 4
    if two_pairs and groups > 1 and by_heads and by_rows:
        return head_shards(count, groups, gate_input, *others)
    return general_shards(gate_input, *others)


def solution(mesh):
    in_specs = (
        P(("groups", "seq"), "chan"),
        P(("groups", "seq"), "chan"),
        P("chan", None),
        P("seq", "chan"),
        P("chan", None, None),
        P(("groups", "seq"), "chan"),
        P(("groups", "seq"), "chan"),
    )
    out_specs = P(("groups", "seq"), "chan")
    return jax.shard_map(
        functools.partial(shards, mesh.shape["seq"], mesh.shape["groups"]), mesh=mesh, in_specs=in_specs, out_specs=out_specs, check_vma=False)
```

```python
import functools
import math

import jax
import jax.numpy as jnp
import numpy as np
from jax import lax
from jax.experimental import pallas as pl
from jax.experimental.pallas import tpu as pltpu
from jax.sharding import PartitionSpec as P

HEAD_DIM = 128
TAPS = 128
RADIX = 128


HIGHEST = lax.Precision.HIGHEST


def shifted(value, axis, steps):
    count = lax.axis_size(axis)
    initial, last = (max(0, -steps), min(count, count - steps))
    return lax.ppermute(value, axis, [(source, source + steps) for source in range(initial, last)])


def unit_table(height, breadth, modulus, orient):
    product = (
        lax.broadcasted_iota(jnp.int32, (height, breadth), 0)
        * lax.broadcasted_iota(jnp.int32, (height, breadth), 1)
        % modulus
    )
    angles = 2.0 * math.pi / modulus * product.astype(jnp.float32)
    return (jnp.cos(angles), orient * jnp.sin(angles))


def block_table(factor, orient):
    inner_re, inner_im = unit_table(factor, factor, factor, orient)
    upper = jnp.concatenate([inner_re, inner_im], axis=1)
    lower = jnp.concatenate([-inner_im, inner_re], axis=1)
    return jnp.concatenate([upper, lower], axis=0)


def spectrum(signal, factor):
    channels, length = signal.shape
    full_length = 2 * length
    column_count = full_length // factor
    folded = signal.reshape(channels, column_count // 2, factor)
    outer_re, outer_im = unit_table(column_count, column_count // 2, column_count, -1.0)
    outer_both = jnp.concatenate([outer_re, outer_im], axis=0)
    first = jnp.einsum("kn,cnm->ckm", outer_both, folded, precision=HIGHEST)
    first_re = first[:, :column_count]
    first_im = first[:, column_count:]
    twist_re, twist_im = unit_table(column_count, factor, full_length, -1.0)
    mid_re = first_re * twist_re - first_im * twist_im
    mid_im = first_re * twist_im + first_im * twist_re
    joined = jnp.concatenate([mid_re, mid_im], axis=2)
    return jnp.einsum("ckn,nm->ckm", joined, block_table(factor, -1.0), precision=HIGHEST)


def inverse(spec_both, factor, length):
    channels = spec_both.shape[0]
    full_length = 2 * length
    column_count = full_length // factor
    mid = jnp.einsum("ckm,mn->ckn", spec_both, block_table(factor, 1.0), precision=HIGHEST)
    mid_re = mid[:, :, :factor]
    mid_im = mid[:, :, factor:]
    twist_re, twist_im = unit_table(column_count, factor, full_length, 1.0)
    turn_re = mid_re * twist_re - mid_im * twist_im
    turn_im = mid_re * twist_im + mid_im * twist_re
    outer_re, outer_im = unit_table(column_count // 2, column_count, column_count, 1.0)
    outer_both = jnp.concatenate([outer_re, -outer_im], axis=1)
    turned = jnp.concatenate([turn_re, turn_im], axis=1)
    result = jnp.einsum("nk,ckm->cnm", outer_both, turned, precision=HIGHEST)
    return result.reshape(channels, length) / full_length


def general_shards(
    gate_input, value_input, short_filter, long_filter, query_weight, key_matrix, value_matrix
):
    seq_rows, local_width = gate_input.shape
    last_rows = gate_input[seq_rows - (TAPS - 1) :]
    earlier = shifted(last_rows, "seq", 1)
    padded = jnp.concatenate([earlier, gate_input], axis=0).astype(jnp.float32)
    kernel = short_filter[:, ::-1].T[:, None, :]
    smoothed = lax.conv_general_dilated(
        padded[None],
        kernel,
        (1,),
        "VALID",
        dimension_numbers=("NHC", "HIO", "NHC"),
        feature_group_count=local_width,
        precision=HIGHEST,
    )[0]
    mixed_input = (smoothed * value_input.astype(jnp.float32)).astype(jnp.bfloat16)
    signal, kernel_line = (
        lax.all_to_all(mixed_input.T, "seq", split_axis=0, concat_axis=1, tiled=True),
        lax.all_to_all(long_filter.T, "seq", split_axis=0, concat_axis=1, tiled=True),
    )
    length = signal.shape[1]
    signal_both = spectrum(signal.astype(jnp.float32), RADIX)
    kernel_both = spectrum(kernel_line.astype(jnp.float32), RADIX)
    signal_re = signal_both[:, :, :RADIX]
    signal_im = signal_both[:, :, RADIX:]
    kernel_re = kernel_both[:, :, :RADIX]
    kernel_im = kernel_both[:, :, RADIX:]
    joint = jnp.concatenate(
        [
            signal_re * kernel_re - signal_im * kernel_im,
            signal_re * kernel_im + signal_im * kernel_re,
        ],
        axis=2,
    )
    conv_line = inverse(joint, RADIX, length).astype(jnp.bfloat16)
    my_index = lax.axis_index("seq")
    group_firsts = [my_index * seq_rows]
    conv_columns = lax.all_to_all(conv_line, "seq", split_axis=1, concat_axis=0, tiled=True)
    heads_here = local_width // HEAD_DIM
    conv_heads = conv_columns.reshape(heads_here, HEAD_DIM, seq_rows)
    query_heads = jnp.einsum(
        "hds,hde->hse", conv_heads, query_weight, preferred_element_type=jnp.float32
    ).astype(jnp.bfloat16)
    group_count = len(group_firsts)
    query_groups = [query_heads]
    key_heads = key_matrix.reshape(seq_rows, heads_here, HEAD_DIM).transpose(1, 0, 2)
    value_heads = value_matrix.reshape(seq_rows, heads_here, HEAD_DIM).transpose(1, 0, 2)
    score_scale = 1.0 / math.sqrt(HEAD_DIM)

    def attend_group(running, group_query, group_first, key_block, value_block, first_row):
        block_rows = key_block.shape[1]

        def compute(current):
            peak_value, weight_sum, weighted = current
            scores = (
                jnp.einsum(
                    "hqd,hkd->hqk", group_query, key_block, preferred_element_type=jnp.float32
                )
                * score_scale
            )
            key_pos = first_row + lax.iota(jnp.int32, block_rows)
            query_pos = group_first + lax.iota(jnp.int32, seq_rows)
            allowed = (key_pos[None, :] <= query_pos[:, None])[None]
            scores = jnp.where(allowed, scores, -1e30)
            new_peak = jnp.maximum(peak_value, jnp.max(scores, axis=2))
            weights = jnp.where(allowed, jnp.exp(scores - new_peak[:, :, None]), 0.0)
            rescale = jnp.exp(peak_value - new_peak)
            weight_sum = weight_sum * rescale + jnp.sum(weights, axis=2)
            weighted = weighted * rescale[:, :, None] + jnp.einsum(
                "hqk,hkd->hqd",
                weights.astype(jnp.bfloat16),
                value_block,
                preferred_element_type=jnp.float32,
            )
            return (new_peak, weight_sum, weighted)

        live = first_row <= group_first + seq_rows - 1
        return lax.cond(live, compute, lambda current: current, running)

    def attend(states, key_block, value_block, first_row):
        return tuple(
            (
                attend_group(
                    states[g], query_groups[g], group_firsts[g], key_block, value_block, first_row
                )
                for g in range(group_count)
            )
        )

    one_state = (
        jnp.full((heads_here, seq_rows), -1e30, jnp.float32),
        jnp.zeros((heads_here, seq_rows), jnp.float32),
        jnp.zeros((heads_here, seq_rows, HEAD_DIM), jnp.float32),
    )
    initial = tuple((one_state for g in range(group_count)))
    running = initial
    key_piece = lax.all_gather(key_heads, "seq", axis=1, tiled=True)
    value_piece = lax.all_gather(value_heads, "seq", axis=1, tiled=True)
    piece_rows = key_piece.shape[1]
    block_rows = 512
    block_count = piece_rows // block_rows
    key_blocks = key_piece.reshape(heads_here, block_count, block_rows, HEAD_DIM).transpose(
        1, 0, 2, 3
    )
    value_blocks = value_piece.reshape(heads_here, block_count, block_rows, HEAD_DIM).transpose(
        1, 0, 2, 3
    )

    def advance(current, element):
        key_block, value_block, position = element
        return (attend(current, key_block, value_block, position * block_rows), None)

    running, _ = lax.scan(
        advance, running, (key_blocks, value_blocks, lax.iota(jnp.int32, block_count))
    )
    outputs = [state[2] / state[1][:, :, None] for state in running]
    result = outputs[0]
    attended_rows = result.transpose(1, 0, 2).reshape(seq_rows, local_width).astype(jnp.bfloat16)
    return attended_rows


def split_pair(array):
    high = array.astype(jnp.bfloat16)
    return high, (array - high.astype(jnp.float32)).astype(jnp.bfloat16)


def transform_tables(rows):
    full = 2 * rows
    turn = np.arange(rows)[:, None] * np.arange(full)[None, :] % full
    angle = 2.0 * np.pi / full * turn
    forward = np.concatenate([np.cos(angle), -np.sin(angle)], axis=0)
    forward[rows] = 1.0 - 2.0 * (np.arange(full) % 2)
    weight = np.full((full,), 2.0 / full)
    weight[0] = weight[rows] = 1.0 / full
    backward = (forward[:, :rows] * weight[:, None]).T
    return forward, backward


def host_split(table):
    high = table.astype(jnp.bfloat16)
    low = (table - high.astype(np.float64)).astype(jnp.bfloat16)
    return jnp.asarray(high), jnp.asarray(low)


def dot(a, b, contract=((1,), (0,))):
    return lax.dot_general(a, b, (contract, ((), ())), preferred_element_type=jnp.float32)


def block_kernel(
    count,
    gate_in,
    value_in,
    long_in,
    key_in,
    val_in,
    short_in,
    weight_in,
    fwd_high_in,
    fwd_low_in,
    inv_high_in,
    inv_low_in,
    out,
    held,
    short_taps,
    head_weight,
    fwd_high,
    fwd_low,
    inv_high,
    inv_low,
    grid_re,
    grid_im,
    grid_nyq,
    sig_re,
    sig_im,
    conv,
    weights,
    sums,
    result,
    smoothed,
    mixed,
    far_taps,
    far_gate,
    far_before,
    far_value,
    far_mixed,
    halo_sem,
    pass_send,
    pass_recv,
    send_sem,
    recv_sem,
    own_sem,
    out_send,
    out_recv,
    out_own,
    table_sem,
):
    me = lax.axis_index("seq")
    rows = gate_in.shape[0]
    width = held.shape[2]
    heads = width // HEAD_DIM
    streams = (gate_in, value_in, long_in, key_in, val_in)
    GATE, VALUE, LONG, KEY, VAL = range(5)
    groups = lax.axis_size("groups")
    my_group = lax.axis_index("groups")
    share = width // groups

    def flip(index):
        return index + 1 - 2 * lax.rem(index, 2)

    partner = flip(me)
    opposite = lax.rem(me + 2, count)
    far = [opposite, flip(opposite)]
    peers = [*far, partner]
    late = me // 2
    far_columns = pl.ds(pl.multiple_of((1 - late) * 2 * width, 2 * width), 2 * width)

    tables = [
        pltpu.make_async_copy(source, target, table_sem.at[i])
        for i, (source, target) in enumerate(
            (
                (fwd_high_in, fwd_high),
                (fwd_low_in, fwd_low),
                (inv_high_in, inv_high),
                (inv_low_in, inv_low),
                (short_in.at[pl.ds(pl.multiple_of(me * width, width), width)], short_taps),
                (short_in.at[far_columns], far_taps),
                (gate_in.at[:, far_columns], far_gate),
                (value_in.at[:, far_columns], far_value),
                (weight_in.at[pl.ds(me * heads, heads)], head_weight),
            )
        )
    ]
    for copy in tables:
        copy.start()
    my_rows = pl.ds(pl.multiple_of(me * rows, rows), rows)
    my_columns = pl.ds(pl.multiple_of(me * width, width), width)
    own = [
        pltpu.make_async_copy(stream.at[:, my_columns], held.at[a, my_rows], own_sem.at[a])
        for a, stream in enumerate(streams)
    ]
    for copy in own:
        copy.start()

    barrier = pltpu.get_barrier_semaphore()
    siblings = [lax.rem(my_group + step, groups) for step in range(1, groups)]
    for peer in peers:
        pl.semaphore_signal(
            barrier, inc=1, device_id={"seq": peer}, device_id_type=pl.DeviceIdType.MESH
        )
    for sibling in siblings:
        pl.semaphore_signal(
            barrier, inc=1, device_id={"groups": sibling}, device_id_type=pl.DeviceIdType.MESH
        )
    pl.semaphore_wait(barrier, len(peers) + len(siblings))

    def block_of(index):
        return pl.ds(pl.multiple_of(index * rows, rows), rows)

    def exchange(a, slot, peer, source, first, breadth):
        there = pl.ds(pl.multiple_of(peer * width + first, HEAD_DIM), breadth)
        here = pl.ds(pl.multiple_of(first, HEAD_DIM), breadth)
        return pltpu.make_async_remote_copy(
            src_ref=streams[a].at[:, there],
            dst_ref=held.at[a, block_of(source), here],
            send_sem=send_sem.at[slot, peer],
            recv_sem=recv_sem.at[slot, source],
            device_id={"seq": peer},
            device_id_type=pl.DeviceIdType.MESH,
        )

    def pass_on(step, source):
        here = pl.ds(pl.multiple_of(my_group * share, HEAD_DIM), share)
        return pltpu.make_async_remote_copy(
            src_ref=held.at[LONG, block_of(source), here],
            dst_ref=held.at[LONG, block_of(source), here],
            send_sem=pass_send.at[step, source],
            recv_sem=pass_recv.at[step, source],
            device_id={"groups": siblings[step]},
            device_id_type=pl.DeviceIdType.MESH,
        )

    def long_part(peer):
        return (0, width) if peer is partner else (my_group * share, share)

    halo = pltpu.make_async_remote_copy(
        src_ref=gate_in.at[:, far_columns],
        dst_ref=far_before,
        send_sem=halo_sem.at[0],
        recv_sem=halo_sem.at[1],
        device_id={"seq": partner},
        device_id_type=pl.DeviceIdType.MESH,
    )

    def send_mixed(peer, source):
        there = pl.ds(pl.multiple_of(lax.rem(peer, 2) * width, width), width)
        return pltpu.make_async_remote_copy(
            src_ref=far_mixed.at[:, there],
            dst_ref=mixed.at[block_of(source)],
            send_sem=send_sem.at[3, peer],
            recv_sem=recv_sem.at[3, source],
            device_id={"seq": peer},
            device_id_type=pl.DeviceIdType.MESH,
        )

    @pl.when(lax.rem(me, 2) == 0)
    def _():
        halo.start()

    sent = []
    for peer in peers:
        sent.append(exchange(LONG, 0, peer, me, *long_part(peer)))
    for a, slot in ((GATE, 1), (VALUE, 2)):
        sent.append(exchange(a, slot, partner, me, 0, width))
    for copy in sent:
        copy.start()
    raw_gate = [exchange(GATE, 1, peer, me, 0, width) for peer in far]
    raw_value = [exchange(VALUE, 2, peer, me, 0, width) for peer in far]
    sent_mixed = [send_mixed(peer, me) for peer in far]
    sends_gate = jnp.logical_or(me == 1, me == 2)
    sends_value = me == 2

    @pl.when(sends_gate)
    def _():
        for copy in raw_gate:
            copy.start()

    @pl.when(sends_value)
    def _():
        for copy in raw_value:
            copy.start()

    def arrive(a, slot, first=0, breadth=width):
        for peer in peers:
            exchange(a, slot, peer, peer, first, breadth).wait_recv()

    for copy in tables:
        copy.wait()

    def forward(signal):
        depth = signal.shape[0]
        both = dot(fwd_high[:, :depth], signal) + dot(fwd_low[:, :depth], signal)
        return both[:rows], both[rows:]

    def backward(re, im):
        re_high, re_low = split_pair(re)
        im_high, im_low = split_pair(im)
        high = jnp.concatenate([re_high, im_high], axis=0)
        low = jnp.concatenate([re_low, im_low], axis=0)
        return dot(inv_high[...], high) + (dot(inv_low[...], high) + dot(inv_high[...], low))

    def factor_parts(re, im):
        first = lax.broadcasted_iota(jnp.int32, re.shape, 0) == 0
        return re, jnp.where(first, 0.0, im), jnp.where(first, im, re)

    def window(a, block):
        now = held[a, block * rows : (block + 1) * rows]
        if block == 0:
            return now
        return jnp.concatenate([now, held[a, (block - 1) * rows : block * rows]], axis=0)

    last = ((1,), (1,))

    def taps_parts(taps):
        high, low = split_pair(taps[...])
        both = dot(fwd_high[:, :TAPS], high, last) + (
            dot(fwd_low[:, :TAPS], high, last) + dot(fwd_high[:, :TAPS], low, last)
        )
        return factor_parts(both[:rows], both[rows:])

    def smooth(signal, parts):
        re, im = forward(signal)
        re_part, im_part, nyq_part = parts
        return backward(re * re_part - im * im_part, re * im_part + im * nyq_part)

    @pl.when(me == 0)
    def _():
        far_before[...] = jnp.zeros_like(far_before)

    @pl.when(jnp.logical_not(sends_value))
    def _():
        far_parts = taps_parts(far_taps)

        @pl.when(lax.rem(me, 2) == 1)
        def _():
            halo.wait_recv()

        filtered = smooth(jnp.concatenate([far_gate[...], far_before[...]], axis=0), far_parts)
        far_mixed[...] = (filtered * far_value[...].astype(jnp.float32)).astype(jnp.bfloat16)
        for copy in sent_mixed:
            copy.start()

    late_sent = []
    for head in range(heads):
        for a, slot in ((KEY, 4 + 2 * head), (VAL, 5 + 2 * head)):
            for peer in peers:
                late_sent.append(exchange(a, slot, peer, me, head * HEAD_DIM, HEAD_DIM))
    for copy in late_sent:
        copy.start()

    passed = []
    for peer in peers:
        exchange(LONG, 0, peer, peer, *long_part(peer)).wait_recv()
        if peer is not partner:
            for step in range(groups - 1):
                passed.append(pass_on(step, peer))
                passed[-1].start()

    parts = taps_parts(short_taps)
    own[GATE].wait()
    for source in (partner, 2 - late):
        exchange(GATE, 1, source, source, 0, width).wait_recv()

    def smooth_blocks(*blocks):
        for block in blocks:
            smoothed[block] = smooth(window(GATE, block), parts)

    def mix_blocks(*blocks):
        for block in blocks:
            here = slice(block * rows, (block + 1) * rows)
            mixed[here] = (smoothed[block] * held[VALUE, here].astype(jnp.float32)).astype(
                jnp.bfloat16
            )

    smooth_blocks(2)

    @pl.when(late == 0)
    def _():
        smooth_blocks(0, 1)

    @pl.when(late == 1)
    def _():
        smooth_blocks(3)

    own[LONG].wait()
    for copy in passed:
        copy.wait_recv()
    for block in range(count):
        re, im, nyq = factor_parts(*forward(window(LONG, block)))
        grid_re[block], grid_im[block], grid_nyq[block] = re, im, nyq

    own[VALUE].wait()
    exchange(VALUE, 2, partner, partner, 0, width).wait_recv()

    @pl.when(late == 0)
    def _():
        exchange(VALUE, 2, 2, 2, 0, width).wait_recv()
        mix_blocks(0, 1, 2)
        send_mixed(3, 3).wait_recv()

    @pl.when(late == 1)
    def _():
        mix_blocks(2, 3)
        send_mixed(0, 0).wait_recv()
        send_mixed(1, 1).wait_recv()

    for block in range(count):
        sig_re[block], sig_im[block] = forward(mixed[block * rows : (block + 1) * rows])

    for block in range(count):
        re = im = None
        for source in range(block + 1):
            lag = block - source
            s_re, s_im = sig_re[source], sig_im[source]
            re_term = s_re * grid_re[lag] - s_im * grid_im[lag]
            im_term = s_re * grid_im[lag] + s_im * grid_nyq[lag]
            re = re_term if re is None else re + re_term
            im = im_term if im is None else im + im_term
        conv[block * rows : (block + 1) * rows] = backward(re, im).astype(jnp.bfloat16)

    def give_back(block, head, peer):
        columns = pl.ds(pl.multiple_of(me * width + head * HEAD_DIM, HEAD_DIM), HEAD_DIM)
        return pltpu.make_async_remote_copy(
            src_ref=result.at[head, block * rows : (block + 1) * rows],
            dst_ref=out.at[:, columns],
            send_sem=out_send.at[block, head],
            recv_sem=out_recv.at[me, head],
            device_id={"seq": peer},
            device_id_type=pl.DeviceIdType.MESH,
        )

    def keep(block, head):
        columns = pl.ds(pl.multiple_of(me * width + head * HEAD_DIM, HEAD_DIM), HEAD_DIM)
        return pltpu.make_async_copy(
            result.at[head, block * rows : (block + 1) * rows], out.at[:, columns], out_own.at[head]
        )

    scale = 1.0 / math.sqrt(HEAD_DIM)
    own[KEY].wait()
    own[VAL].wait()
    for head in range(heads):
        columns = slice(head * HEAD_DIM, (head + 1) * HEAD_DIM)
        conv[:, columns] = dot(conv[:, columns], head_weight[head]).astype(jnp.bfloat16)
        arrive(KEY, 4 + 2 * head, head * HEAD_DIM, HEAD_DIM)
        for block in range(count):
            here = slice(block * rows, (block + 1) * rows)
            past = (block + 1) * rows
            scores = dot(conv[here, columns], held[KEY, :past, columns], last) * scale
            key_pos = lax.broadcasted_iota(jnp.int32, scores.shape, 1)
            query_pos = block * rows + lax.broadcasted_iota(jnp.int32, scores.shape, 0)
            allowed = key_pos <= query_pos
            scores = jnp.where(allowed, scores, -1e30)
            peak = jnp.max(scores, axis=1, keepdims=True)
            share = jnp.where(allowed, jnp.exp(scores - peak), 0.0)
            sums[head, here] = jnp.broadcast_to(
                jnp.sum(share, axis=1, keepdims=True), (rows, HEAD_DIM)
            )
            weights[head, here, :past] = share.astype(jnp.bfloat16)

        def finish(block):
            here = slice(block * rows, (block + 1) * rows)
            past = (block + 1) * rows
            columns = slice(head * HEAD_DIM, (head + 1) * HEAD_DIM)
            product = dot(weights[head, here, :past], held[VAL, :past, columns])
            result[head, here] = (product / sums[head, here]).astype(jnp.bfloat16)

            @pl.when(me != block)
            def _():
                give_back(block, head, block).start()

            @pl.when(me == block)
            def _():
                keep(block, head).start()

        def value_from(source):
            exchange(
                VAL, 5 + 2 * head, source, source, head * HEAD_DIM, HEAD_DIM
            ).wait_recv()

        value_from(partner)

        @pl.when(late == 0)
        def _():
            for block in (2, 3):
                value_from(block)
                finish(block)
            finish(1)
            finish(0)

        @pl.when(late == 1)
        def _():
            for block in (0, 1):
                value_from(block)
                finish(block)
            finish(2)
            finish(3)

    for copy in [*sent, *passed, *late_sent]:
        copy.wait_send()

    @pl.when(lax.rem(me, 2) == 0)
    def _():
        halo.wait_send()

    @pl.when(sends_gate)
    def _():
        for copy in raw_gate:
            copy.wait_send()

    @pl.when(sends_value)
    def _():
        for copy in raw_value:
            copy.wait_send()

    @pl.when(jnp.logical_not(sends_value))
    def _():
        for copy in sent_mixed:
            copy.wait_send()

    for head in range(heads):
        for peer in peers:
            columns = pl.ds(pl.multiple_of(peer * width + head * HEAD_DIM, HEAD_DIM), HEAD_DIM)
            pltpu.make_async_remote_copy(
                src_ref=result.at[head, :rows],
                dst_ref=out.at[:, columns],
                send_sem=out_send.at[0, head],
                recv_sem=out_recv.at[peer, head],
                device_id={"seq": peer},
                device_id_type=pl.DeviceIdType.MESH,
            ).wait_recv()
        for block in range(count):

            @pl.when(me != block)
            def _():
                give_back(block, head, block).wait_send()

            @pl.when(me == block)
            def _():
                keep(block, head).wait()


def head_shards(
    count,
    groups,
    gate_input,
    value_input,
    short_filter,
    long_filter,
    query_weight,
    key_matrix,
    value_matrix,
):
    rows, local_width = gate_input.shape
    width = local_width // count
    heads = width // HEAD_DIM
    length = count * rows
    forward, inverse_table = transform_tables(rows)
    forward = host_split(forward)
    inverse_table = host_split(inverse_table)
    bf16, f32 = jnp.bfloat16, jnp.float32
    return pl.pallas_call(
        functools.partial(block_kernel, count),
        out_shape=pltpu.VMEM((rows, local_width), bf16),
        in_specs=[pl.BlockSpec(memory_space=pl.ANY)] * 11,
        out_specs=pl.BlockSpec(memory_space=pltpu.VMEM),
        scratch_shapes=[
            pltpu.VMEM((5, length, width), bf16),
            pltpu.VMEM((width, TAPS), f32),
            pltpu.VMEM((heads, HEAD_DIM, HEAD_DIM), bf16),
            pltpu.VMEM((2 * rows, 2 * rows), bf16),
            pltpu.VMEM((2 * rows, 2 * rows), bf16),
            pltpu.VMEM((rows, 2 * rows), bf16),
            pltpu.VMEM((rows, 2 * rows), bf16),
            pltpu.VMEM((count, rows, width), f32),
            pltpu.VMEM((count, rows, width), f32),
            pltpu.VMEM((count, rows, width), f32),
            pltpu.VMEM((count, rows, width), f32),
            pltpu.VMEM((count, rows, width), f32),
            pltpu.VMEM((length, width), bf16),
            pltpu.VMEM((heads, length, length), bf16),
            pltpu.VMEM((heads, length, HEAD_DIM), f32),
            pltpu.VMEM((heads, length, HEAD_DIM), bf16),
            pltpu.VMEM((count, rows, width), f32),
            pltpu.VMEM((length, width), bf16),
            pltpu.VMEM((2 * width, TAPS), f32),
            pltpu.VMEM((rows, 2 * width), bf16),
            pltpu.VMEM((rows, 2 * width), bf16),
            pltpu.VMEM((rows, 2 * width), bf16),
            pltpu.VMEM((rows, 2 * width), bf16),
            pltpu.SemaphoreType.DMA((2,)),
            pltpu.SemaphoreType.DMA((groups - 1, count)),
            pltpu.SemaphoreType.DMA((groups - 1, count)),
            pltpu.SemaphoreType.DMA((4 + 2 * heads, count)),
            pltpu.SemaphoreType.DMA((4 + 2 * heads, count)),
            pltpu.SemaphoreType.DMA((5,)),
            pltpu.SemaphoreType.DMA((count, heads)),
            pltpu.SemaphoreType.DMA((count, heads)),
            pltpu.SemaphoreType.DMA((heads,)),
            pltpu.SemaphoreType.DMA((9,)),
        ],
        compiler_params=pltpu.CompilerParams(collective_id=0, has_side_effects=True),
    )(
        gate_input,
        value_input,
        long_filter,
        key_matrix,
        value_matrix,
        short_filter,
        query_weight,
        *forward,
        *inverse_table,
    )


def shards(count, groups, gate_input, *others):
    rows, local_width = gate_input.shape
    by_heads = local_width % (count * groups * HEAD_DIM) == 0
    by_rows = rows >= TAPS and rows % HEAD_DIM == 0
    two_pairs = count == 4
    if two_pairs and groups > 1 and by_heads and by_rows:
        return head_shards(count, groups, gate_input, *others)
    return general_shards(gate_input, *others)


def solution(mesh):
    in_specs = (
        P(("groups", "seq"), "chan"),
        P(("groups", "seq"), "chan"),
        P("chan", None),
        P("seq", "chan"),
        P("chan", None, None),
        P(("groups", "seq"), "chan"),
        P(("groups", "seq"), "chan"),
    )
    out_specs = P(("groups", "seq"), "chan")
    return jax.shard_map(
        functools.partial(shards, mesh.shape["seq"], mesh.shape["groups"]), mesh=mesh, in_specs=in_specs, out_specs=out_specs, check_vma=False)
```
